32 devices in a mesh: groups: 2 (over y), seq: 4 (over z), inner: 2 (over x), head: 2 (over core).
Axes of the slice: x: 2, y: 2, z: 4, core: 2. Of those that a mesh axis runs over, the one named last changes fastest.
Arguments:
- queries: bfloat16 [2048, 32, 128], P(('groups', 'seq', 'inner'), 'head'), parts along dimension 0, as said below
- keys: bfloat16 [2048, 4, 128], P(('groups', 'seq', 'inner'), 'head'), parts along dimension 0
- values: bfloat16 [2048, 4, 128], P(('groups', 'seq', 'inner'), 'head'), parts along dimension 0, may hold values from -6 to 6
- log_decay: float32 [2048, 4], P(('groups', 'seq', 'inner'), 'head'), parts along dimension 0, as said below
- gain: float32 [32, 128], P('head'), may hold values from 0.1 to 1.9
- block_list: int32 [32, 16], P(('groups', 'seq', 'inner')), parts along dimension 0, may hold values from 0 to 15, as said below
Outputs:
- attended: bfloat16 [2048, 32, 128], P(('groups', 'seq', 'inner'), 'head'), parts along dimension 0
The draws below stay inside these ranges and needn't reach their ends.
There are 2 independent parts, one for each index of `groups`. The reference program is written for one: setup_inputs(seed, part) draws one part's arguments, and reference() takes and returns one part's arrays. A program takes and returns all parts, laid end to end along the dimension named above; an argument that names none is the same for every part. Nothing has to cross between parts.
Inputs may be any that keep to these rules, and one draw needn't show every extreme that they name: Keys lie within -6 to 6; queries within -144 to 144. `log_decay`: each entry is below 0. `block_list`: entry 0 of row b is b. The sequence's pieces of 128 tokens fall into segments: piece p belongs to segment p modulo 2. Every entry of row b is a block at or before b in a piece of b's segment.
All inputs are finite; a program needn't handle non-finite values.
Results may differ from the reference program's by a relative error of at most 0.0017.
Values may be sent and summed in bfloat16 or wider, within the bound.
A program may use at most 64 MiB of HBM per device.

```python
import jax
import jax.numpy as jnp
from jax import lax

HEADS = 32
KEY_VALUE_HEADS = 4
DH = 128
BLK = 64
SEL = 16
TOK_DEV = 128
SEQUENCE_TOKENS = 1024
QBLOCKS = 16
N_INNER = 2


def key_field(key):
    base = jax.random.normal(jax.random.fold_in(key, 11), (SEQUENCE_TOKENS, KEY_VALUE_HEADS, DH), jnp.float32)
    return jnp.clip(base, -6.0, 6.0)


def draw_keys(key, part):
    return key_field(key).astype(jnp.bfloat16)


def draw_queries(key, part):
    base = jax.random.normal(jax.random.fold_in(key, 12), (SEQUENCE_TOKENS, HEADS, DH), jnp.float32)
    base = jnp.clip(base, -6.0, 6.0)
    return base.astype(jnp.bfloat16)


def draw_log_decay(key, part):
    order = jax.random.permutation(jax.random.fold_in(key, 21), KEY_VALUE_HEADS)
    fast = order < (KEY_VALUE_HEADS + 1) // 2
    fast_rate = jnp.exp(jax.random.uniform(jax.random.fold_in(key, 22), (KEY_VALUE_HEADS,), jnp.float32, jnp.log(1.0 / 50.0), jnp.log(1.0 / 30.0)))
    speed_ratio = jnp.where(fast, fast_rate, 0.5 / SEQUENCE_TOKENS)
    pieces = SEQUENCE_TOKENS // TOK_DEV
    multiplier_term = jnp.exp(jax.random.uniform(jax.random.fold_in(key, 23), (pieces, KEY_VALUE_HEADS), jnp.float32, jnp.log(0.5), jnp.log(2.0)))
    multiplier_term = jnp.repeat(multiplier_term, TOK_DEV, axis=0)
    random_wobble = jax.random.uniform(jax.random.fold_in(key, 24), (SEQUENCE_TOKENS, KEY_VALUE_HEADS), jnp.float32, 0.5, 1.5)
    marked_positions = jax.random.randint(jax.random.fold_in(key, 25), (3,), 0, SEQUENCE_TOKENS)
    dropped_amounts = jnp.log(jax.random.uniform(jax.random.fold_in(key, 26), (3, KEY_VALUE_HEADS), jnp.float32, 0.5, 0.8))
    sudden_spike = jnp.zeros((SEQUENCE_TOKENS, KEY_VALUE_HEADS), jnp.float32).at[marked_positions].add(dropped_amounts)
    return -speed_ratio[None, :] * multiplier_term * random_wobble + sudden_spike


def draw_block_list(key, part):
    per_piece = TOK_DEV // BLK
    number = jnp.arange(QBLOCKS)
    piece = number // per_piece
    within = number % per_piece
    outer = piece // N_INNER
    inner_idx = piece % N_INNER
    count = outer * per_piece + within + 1
    raw = jax.random.randint(jax.random.fold_in(key, 31), (QBLOCKS, SEL), 0, 2 ** 30)
    pick = raw % count[:, None]
    chosen = (pick // per_piece * N_INNER + inner_idx[:, None]) * per_piece + pick % per_piece
    chosen = chosen.at[:, 0].set(number)
    return chosen.astype(jnp.int32)


def level_of(stream_key, extent, cuts, least, top_value):
    factor_of = 1.0
    for axis_at, shards_of in cuts:
        draws = jax.random.uniform(jax.random.fold_in(jax.random.fold_in(stream_key, 6), axis_at), (shards_of,), jnp.float32, least / len(cuts), top_value / len(cuts))
        factor_of = factor_of * jnp.repeat(jnp.exp(draws), extent[axis_at] // shards_of).reshape((-1,) + (1,) * (len(extent) - 1 - axis_at))
    return factor_of


def gaussian(own_key, shape, deviation, reach, shards=(), dtype=jnp.bfloat16):
    array = jax.random.normal(own_key, shape, jnp.float32) * deviation
    if len(shards) > 0:
        array = level_of(own_key, shape, shards, -0.22, 0.18) * array
    return jnp.clip(array, min=-reach, max=reach).astype(dtype)


def setup_inputs(seed: int = 0, part: int = 0) -> dict:
    streams_of = jax.random.split(jax.random.key(seed), 7)
    part_splits = jax.random.split(jax.random.fold_in(streams_of[6], part), 7)
    queries = draw_queries(jax.random.fold_in(jax.random.fold_in(streams_of[6], part), 71), part)
    keys = draw_keys(jax.random.fold_in(jax.random.fold_in(streams_of[6], part), 71), part)
    values = gaussian(part_splits[2], (SEQUENCE_TOKENS, KEY_VALUE_HEADS, DH), 1.0, 6.0, ((0, 8), (1, 2)))
    log_decay = draw_log_decay(jax.random.fold_in(jax.random.fold_in(streams_of[6], part), 71), part)
    gain = jnp.clip(1.0 + 0.18 * jax.random.normal(streams_of[4], (HEADS, DH), jnp.float32), 0.1, 1.9)
    block_list = draw_block_list(jax.random.fold_in(jax.random.fold_in(streams_of[6], part), 71), part)
    return dict(queries=queries, keys=keys, values=values, log_decay=log_decay, gain=gain, block_list=block_list)


HIGH = lax.Precision.HIGHEST

def linear_branch(queries, keys, values, log_decay):
    rep = HEADS // KEY_VALUE_HEADS
    count = SEQUENCE_TOKENS // TOK_DEV
    qall = queries.astype(jnp.float32).reshape(count, TOK_DEV, KEY_VALUE_HEADS, rep, DH)
    kall = keys.astype(jnp.float32).reshape(count, TOK_DEV, KEY_VALUE_HEADS, DH)
    vall = values.astype(jnp.float32).reshape(count, TOK_DEV, KEY_VALUE_HEADS, DH)
    dall = log_decay.reshape(count, TOK_DEV, KEY_VALUE_HEADS)
    causal = jnp.arange(TOK_DEV)[:, None] >= jnp.arange(TOK_DEV)[None, :]

    def step(state, piece):
        qf, kf, vf, dec = piece
        cum = jnp.cumsum(dec, axis=0)
        total = cum[-1]
        scores = jnp.einsum('tkrd,skd->krts', qf, kf, precision=HIGH)
        diff = cum.T[:, :, None] - cum.T[:, None, :]
        weight = jnp.where(causal[None], jnp.exp(jnp.minimum(diff, 0.0)), 0.0)
        intra = jnp.einsum('krts,skd->tkrd', scores * weight[:, None], vf, precision=HIGH)
        inter = jnp.exp(cum)[:, :, None, None] * jnp.einsum('tkrd,kde->tkre', qf, state, precision=HIGH)
        tail = jnp.exp(total[None, :] - cum)
        own_state = jnp.einsum('skd,ske->kde', kf * tail[:, :, None], vf, precision=HIGH)
        new_state = jnp.exp(total)[:, None, None] * state + own_state
        return (new_state, (intra + inter).reshape(TOK_DEV, HEADS, DH))
    start = jnp.zeros((KEY_VALUE_HEADS, DH, DH), jnp.float32)
    final_state, pieces = lax.scan(step, start, (qall, kall, vall, dall))
    return pieces.reshape(SEQUENCE_TOKENS, HEADS, DH)

def sparse_branch(queries, keys, values, block_list):
    rep = HEADS // KEY_VALUE_HEADS
    kblocks = keys.astype(jnp.float32).reshape(QBLOCKS, BLK, KEY_VALUE_HEADS, DH)
    vblocks = values.astype(jnp.float32).reshape(QBLOCKS, BLK, KEY_VALUE_HEADS, DH)
    qblocks = queries.astype(jnp.float32).reshape(QBLOCKS, BLK, KEY_VALUE_HEADS, rep, DH)
    lower = jnp.arange(SEL)[None, :] < jnp.arange(SEL)[:, None]

    def one_block(args):
        qblk, sel, number = args
        pk = kblocks[sel]
        pv = vblocks[sel]
        repeat = jnp.any((sel[:, None] == sel[None, :]) & lower, axis=1)
        keep = jnp.logical_not(repeat)
        qpos = number * BLK + jnp.arange(BLK)
        kpos = sel[:, None] * BLK + jnp.arange(BLK)[None, :]
        valid = keep[None, :, None] & (kpos[None] <= qpos[:, None, None])
        score = jnp.einsum('qkrd,jukd->krqju', qblk, pk, precision=HIGH) * DH ** (-0.5)
        score = jnp.where(valid[None, None], score, -1e+30)
        top = lax.optimization_barrier(jnp.max(score, axis=(3, 4), keepdims=True))
        expo = jnp.where(valid[None, None], jnp.exp(score - top), 0.0)
        denom = lax.optimization_barrier(jnp.sum(expo, axis=(3, 4)))
        weights = expo.astype(jnp.bfloat16).astype(jnp.float32)
        out = jnp.einsum('krqju,jukd->qkrd', weights, pv, precision=HIGH)
        return out / jnp.transpose(denom, (2, 0, 1))[:, :, :, None]
    numbers = jnp.arange(QBLOCKS).astype(jnp.int32)
    outs = lax.map(one_block, (qblocks, block_list, numbers))
    return outs.reshape(SEQUENCE_TOKENS, HEADS, DH)

def reference(queries, keys, values, log_decay, gain, block_list):
    linear = linear_branch(queries, keys, values, log_decay)
    normed = linear * lax.rsqrt(lax.optimization_barrier(jnp.mean(linear * linear, axis=-1, keepdims=True)) + 1e-06) * gain[None]
    sparse = sparse_branch(queries, keys, values, block_list)
    return (normed + sparse).astype(jnp.bfloat16)
```

```python
import functools

import jax
import jax.numpy as jnp
from jax import lax
from jax.experimental import pallas as pl
from jax.experimental.pallas import tpu as pltpu
from jax.sharding import PartitionSpec as P

BLK = 64
HIGH = lax.Precision.HIGHEST
MESH = pl.DeviceIdType.MESH
LD_ROWS = 8
F32 = jnp.float32
BF16 = jnp.bfloat16
LOG2E = 1.4426950408889634


def iota(shape, dim):
    return lax.broadcasted_iota(jnp.int32, shape, dim)


def dot(a, b, dims=((1,), (0,)), precision=None):
    return lax.dot_general(
        a, b, (dims, ((), ())), precision=precision, preferred_element_type=F32
    )


def halves(x):
    hi = x.astype(BF16)
    return hi, (x - hi.astype(F32)).astype(BF16)


def kernel(
    n_seq, n_inner, kv,
    q_hbm, k_hbm, v_hbm, ld_hbm, gain_hbm, list_hbm,
    out_ref,
    gain_ref, list_ref, qbuf, kbuf, vbuf, ldbuf, qs, kd, vd, bias, lin, sp, msg, got, own_msg, own_got,
    local_sem, k_send, k_recv, v_send, v_recv, l_send, l_recv, x_send, x_recv,
    m_send, m_recv, o_send, o_recv,
):
    z = lax.axis_index("seq")
    x = lax.axis_index("inner")
    tokens, heads, width = qbuf.shape
    rep = heads // kv
    rows = tokens * rep
    per_piece = tokens // BLK
    keys_all = n_seq * tokens
    has_next, has_last = z < n_seq - 1, z > 0

    q_copy = pltpu.make_async_copy(q_hbm, qbuf, local_sem.at[0])
    k_copy = pltpu.make_async_copy(k_hbm, kbuf.at[0], local_sem.at[1])
    v_copy = pltpu.make_async_copy(v_hbm, vbuf.at[0], local_sem.at[2])
    l_copy = pltpu.make_async_copy(ld_hbm, ldbuf.at[0, 0, 0:kv], local_sem.at[3])
    g_copy = pltpu.make_async_copy(gain_hbm, gain_ref, local_sem.at[4])
    list_copy = pltpu.make_async_copy(list_hbm, list_ref, local_sem.at[5])

    barrier = pltpu.get_barrier_semaphore()
    ldbuf[...] = jnp.zeros_like(ldbuf)

    @pl.when(has_next)
    def _():
        pl.semaphore_signal(barrier, inc=1, device_id={"seq": z + 1}, device_id_type=MESH)

    @pl.when(has_last)
    def _():
        pl.semaphore_signal(barrier, inc=1, device_id={"seq": z - 1}, device_id_type=MESH)

    for o in range(1, n_inner):
        pl.semaphore_signal(
            barrier, inc=1, device_id={"inner": lax.rem(x + o, n_inner)}, device_id_type=MESH)
    for copy in (l_copy, k_copy, v_copy, list_copy, q_copy, g_copy):
        copy.start()
    ends = jnp.where(has_next, 1, 0) + jnp.where(has_last, 1, 0)
    pl.semaphore_wait(barrier, n_inner - 1 + ends)

    def hop(src, dst, send, recv):
        return pltpu.make_async_remote_copy(
            src_ref=src, dst_ref=dst, send_sem=send, recv_sem=recv,
            device_id={"seq": z + 1}, device_id_type=MESH)

    def k_hop(j):
        return hop(
            k_hbm if j == 0 else kbuf.at[j], kbuf.at[j + 1], k_send.at[j], k_recv.at[j + 1])

    def v_hop(j):
        return hop(
            v_hbm if j == 0 else vbuf.at[j], vbuf.at[j + 1], v_send.at[j], v_recv.at[j + 1])

    def l_hop(j):
        return hop(
            ldbuf.at[j, :, 0:kv], ldbuf.at[j + 1, :, 0:kv], l_send.at[j], l_recv.at[j + 1])

    def relay(hops, j):
        @pl.when(z >= j)
        def _():
            hops(j - 1).wait_recv()

        if j < n_seq - 1:

            @pl.when((z >= j) & has_next)
            def _():
                hops(j).start()

    def x_copy(o):
        return pltpu.make_async_remote_copy(
            src_ref=ld_hbm, dst_ref=ldbuf.at[0, n_inner - o, 0:kv], send_sem=x_send.at[o],
            recv_sem=x_recv.at[o], device_id={"inner": lax.rem(x + o, n_inner)},
            device_id_type=MESH)

    @pl.when(has_next)
    def _():
        k_hop(0).start()
        v_hop(0).start()

    for o in range(1, n_inner):
        x_copy(o).start()

    lanes = iota((kv * tokens, kv * tokens), 1)
    subs = iota((kv * tokens, kv * tokens), 0)
    by_head = jnp.where(
        lanes == lax.rem(subs, tokens) * kv + subs // tokens, 1.0, 0.0
    ).astype(BF16)

    l_copy.wait()
    ld = ldbuf[0, 0]
    upto = jnp.where(iota((tokens, tokens), 0) <= iota((tokens, tokens), 1), 1.0, 0.0)
    after = jnp.where(iota((tokens, tokens), 0) < iota((tokens, tokens), 1), 1.0, 0.0)
    cum_lane = dot(ld, upto, precision=HIGH)
    row_tok = iota((rows, tokens), 0) // rep
    lane_tok = iota((rows, tokens), 1)
    seen = row_tok >= lane_tok
    cum_row = dot(jnp.where(seen, 1.0, 0.0), ld, ((1,), (1,)), HIGH)
    own_tail = dot(after, ld, ((1,), (1,)), HIGH)

    def outer(k, weighted):
        hi, lo = halves(weighted)
        return dot(
            jnp.concatenate([k, k], axis=0), jnp.concatenate([hi, lo], axis=0), ((0,), (0,)))

    def split(j):
        k_j = dot(by_head, kbuf[j]).astype(BF16)
        v_j = dot(by_head, vbuf[j])
        out = []
        for g in range(kv):
            k_g = k_j[g * tokens:(g + 1) * tokens]
            v_g = v_j[g * tokens:(g + 1) * tokens]
            kd[g, j * tokens:(j + 1) * tokens, :] = k_g
            vd[g, j * tokens:(j + 1) * tokens, :] = v_g.astype(BF16)
            out.append((k_g, v_g))
        return out

    k_copy.wait()
    v_copy.wait()
    mine = split(0)
    own = [outer(k_g, v_g * jnp.exp(own_tail[:, g:g + 1])) for g, (k_g, v_g) in enumerate(mine)]
    for g in range(kv):
        own_msg[g] = own[g]

    def o_copy(o):
        return pltpu.make_async_remote_copy(
            src_ref=own_msg, dst_ref=own_got.at[o], send_sem=o_send.at[o],
            recv_sem=o_recv.at[o], device_id={"inner": lax.rem(x + o, n_inner)},
            device_id_type=MESH)

    for o in range(1, n_inner):
        x_copy(o).wait_recv()

    @pl.when(has_next)
    def _():
        l_hop(0).start()

    for o in range(1, n_inner):
        o_copy(o).start()

    def visibility():
        key_lane = iota((1, keys_all), 1)
        key_block = (
            ((z - key_lane // tokens) * n_inner + x) * per_piece + lax.rem(key_lane, tokens) // BLK
        )
        key_pos = key_block * BLK + lax.rem(key_lane, BLK)
        list_copy.wait()
        listed = list_ref[...]
        for b in range(per_piece):
            member = key_block == listed[b:b + 1, 0:1]
            for i in range(1, listed.shape[1]):
                member = jnp.logical_or(member, key_block == listed[b:b + 1, i:i + 1])
            limit = jnp.where(member, key_pos, jnp.int32(2**30))
            first = (z * n_inner + x) * tokens + b * BLK
            query = first + iota((BLK * rep, 1), 0) // rep
            bias[b * BLK * rep:(b + 1) * BLK * rep, :] = jnp.where(limit <= query, 0.0, -1e30)

    def take_queries():
        q_copy.wait()
        qf = qbuf[...].astype(F32)
        for g in range(kv):
            qs[g] = qf[:, g * rep:(g + 1) * rep, :].reshape(rows, width).astype(BF16)

    def within(g):
        k_g, v_g = mine[g][0], mine[g][1].astype(BF16)
        diff = cum_row[:, g:g + 1] - cum_lane[g:g + 1, :]
        weight = jnp.where(seen, jnp.exp(jnp.minimum(diff, 0.0)), 0.0)
        hi, lo = halves(dot(qs[g], k_g, ((1,), (1,))) * weight)
        lin[g] = dot(
            jnp.concatenate([hi, lo], axis=1), jnp.concatenate([v_g, v_g], axis=0))

    state = [jnp.zeros((width, width), F32) for _ in range(kv)]
    gap = [jnp.zeros((1, 1), F32) for _ in range(kv)]

    def totals(j):
        t = jnp.sum(ldbuf[j].reshape(n_inner * LD_ROWS, tokens), axis=1, keepdims=True)
        return [[t[o * LD_ROWS + g:o * LD_ROWS + g + 1, :] for o in range(n_inner)]
                for g in range(kv)]

    def absorb(j):
        row = totals(j)
        tail = dot(after, ldbuf[j, 0], ((1,), (1,)), HIGH)
        for g, (k_g, v_g) in enumerate(split(j)):
            rest = gap[g]
            for o in range(1, n_inner):
                rest = rest + jnp.where(x + o < n_inner, row[g][o], 0.0)
            state[g] = state[g] + outer(k_g, v_g * jnp.exp(tail[:, g:g + 1] + rest))
            gap[g] = gap[g] + sum(row[g])

    def first_head():
        take_queries()
        within(0)

    work = [visibility, first_head] + [functools.partial(within, g) for g in range(1, kv)]
    for j in range(1, n_seq):

        @pl.when(z < j)
        def _():
            kbuf[j] = jnp.zeros_like(kbuf[j])
            vbuf[j] = jnp.zeros_like(vbuf[j])

        relay(k_hop, j)
        if work:
            work.pop(0)()
        relay(v_hop, j)
        relay(l_hop, j)
        work.append(functools.partial(absorb, j))
        work.pop(0)()
    for item in work:
        item()

    row = totals(0)
    before = []
    for g in range(kv):
        past, ahead = jnp.zeros((1, 1), F32), jnp.zeros((1, 1), F32)
        for o in range(1, n_inner):
            past = past + jnp.where(x + o >= n_inner, row[g][o], 0.0)
            ahead = ahead + jnp.where(x + o < n_inner, row[g][o], 0.0)
        before.append(past)
        msg[g] = state[g] * jnp.exp(sum(row[g])) + own[g] * jnp.exp(ahead)

    def m_copy(o):
        return pltpu.make_async_remote_copy(
            src_ref=msg, dst_ref=got.at[o], send_sem=m_send.at[o], recv_sem=m_recv.at[o],
            device_id={"seq": z + 1, "inner": lax.rem(x + o, n_inner)}, device_id_type=MESH)

    @pl.when(has_next)
    def _():
        for o in range(1, n_inner):
            m_copy(o).start()

    step = min(rows, 512)
    scale = width ** (-0.5) * LOG2E

    @pl.loop(0, rows // step, unroll=True)
    def _(c):
        at = pl.ds(pl.multiple_of(c * step, step), step)
        for g in range(kv):
            score = dot(qs[g, at, :], kd[g], ((1,), (1,))) + bias[at, :]
            top = jnp.max(score, axis=1, keepdims=True)
            expo = jnp.exp2((score - top) * scale)
            denom = jnp.sum(expo, axis=1, keepdims=True)
            sp[g, at, :] = dot(expo.astype(BF16), vd[g]) / denom


    @pl.when(has_last)
    def _():
        for o in range(1, n_inner):
            m_copy(o).wait_recv()

    @pl.when(z == 0)
    def _():
        got[...] = jnp.zeros_like(got)

    prior = []
    for g in range(kv):
        at_row = state[g]
        for o in range(1, n_inner):
            at_row = at_row + got[o, g]
        prior.append(at_row * jnp.exp(before[g]))
    for o in range(1, n_inner):
        o_copy(o).wait_recv()
        for g in range(kv):
            later = jnp.zeros((1, 1), F32)
            for r in range(n_inner - o + 1, n_inner):
                later = later + row[g][r]
            prior[g] = prior[g] + own_got[o, g] * jnp.where(x >= o, jnp.exp(later), 0.0)

    g_copy.wait()
    done = []
    for g in range(kv):
        hi, lo = halves(prior[g])
        q_g = qs[g]
        inter = dot(
            jnp.concatenate([q_g, q_g], axis=1), jnp.concatenate([hi, lo], axis=0))
        linear = lin[g] + inter * jnp.exp(cum_row[:, g:g + 1])
        norm = lax.rsqrt(jnp.mean(linear * linear, axis=1, keepdims=True) + 1e-6)
        scaled = (linear * norm).reshape(tokens, rep, width) * gain_ref[g * rep:(g + 1) * rep, :][None]
        done.append(scaled + sp[g].reshape(tokens, rep, width))
    out_ref[...] = jnp.concatenate(done, axis=1).astype(out_ref.dtype)

    for j in range(n_seq - 1):

        @pl.when((z >= j) & has_next)
        def _():
            for hops in (k_hop, v_hop, l_hop):
                hops(j).wait_send()

    for o in range(1, n_inner):
        x_copy(o).wait_send()
        o_copy(o).wait_send()

    @pl.when(has_next)
    def _():
        for o in range(1, n_inner):
            m_copy(o).wait_send()


def shards(n_seq, n_inner, queries, keys, values, log_decay, gain, block_list):
    tokens, heads, width = queries.shape
    kv = keys.shape[1]
    rows = tokens * (heads // kv)
    vmem = pl.BlockSpec(memory_space=pltpu.VMEM)
    anywhere = pl.BlockSpec(memory_space=pl.ANY)
    dma = pltpu.SemaphoreType.DMA
    return pl.pallas_call(
        functools.partial(kernel, n_seq, n_inner, kv),
        out_shape=pltpu.VMEM(queries.shape, queries.dtype),
        in_specs=[anywhere] * 6,
        out_specs=vmem,
        scratch_shapes=[
            pltpu.VMEM(gain.shape, F32),
            pltpu.VMEM(block_list.shape, jnp.int32),
            pltpu.VMEM(queries.shape, BF16),
            pltpu.VMEM((n_seq, kv * tokens, width), BF16),
            pltpu.VMEM((n_seq, kv * tokens, width), BF16),
            pltpu.VMEM((n_seq, n_inner, LD_ROWS, tokens), F32),
            pltpu.VMEM((kv, rows, width), BF16),
            pltpu.VMEM((kv, n_seq * tokens, width), BF16),
            pltpu.VMEM((kv, n_seq * tokens, width), BF16),
            pltpu.VMEM((rows, n_seq * tokens), F32),
            pltpu.VMEM((kv, rows, width), F32),
            pltpu.VMEM((kv, rows, width), F32),
            pltpu.VMEM((kv, width, width), F32),
            pltpu.VMEM((n_inner, kv, width, width), F32),
            pltpu.VMEM((kv, width, width), F32),
            pltpu.VMEM((n_inner, kv, width, width), F32),
            dma((6,)),
            dma((n_seq,)), dma((n_seq,)), dma((n_seq,)), dma((n_seq,)),
            dma((n_seq,)), dma((n_seq,)), dma((n_inner,)), dma((n_inner,)),
            dma((n_inner,)), dma((n_inner,)), dma((n_inner,)), dma((n_inner,)),
        ],
        compiler_params=pltpu.CompilerParams(collective_id=0, has_side_effects=True),
        name="prefill",
    )(
        queries, keys.reshape(tokens * kv, width), values.reshape(tokens * kv, width),
        log_decay.T, gain, block_list,
    )


def solution(mesh):
    return jax.shard_map(
        functools.partial(shards, mesh.shape["seq"], mesh.shape["inner"]),
        mesh=mesh,
        in_specs=(
            P(("groups", "seq", "inner"), "head", None),
            P(("groups", "seq", "inner"), "head", None),
            P(("groups", "seq", "inner"), "head", None),
            P(("groups", "seq", "inner"), "head"),
            P("head", None),
            P(("groups", "seq", "inner"), None),
        ),
        out_specs=P(("groups", "seq", "inner"), "head", None),
        check_vma=False,
    )
```

```python
import functools

import jax
import jax.numpy as jnp
from jax import lax
from jax.experimental import pallas as pl
from jax.experimental.pallas import tpu as pltpu
from jax.sharding import PartitionSpec as P

BLK = 64
HIGH = lax.Precision.HIGHEST
MESH = pl.DeviceIdType.MESH
LD_ROWS = 8
F32 = jnp.float32
BF16 = jnp.bfloat16
LOG2E = 1.4426950408889634
NEVER = -1e30


def iota(shape, dim):
    return lax.broadcasted_iota(jnp.int32, shape, dim)


def dot(a, b, dims=((1,), (0,)), precision=None):
    return lax.dot_general(
        a, b, (dims, ((), ())), precision=precision, preferred_element_type=F32
    )


def halves(x):
    hi = x.astype(BF16)
    return hi, (x - hi.astype(F32)).astype(BF16)


def thirds(x):
    hi = x.astype(BF16)
    rest = x - hi.astype(F32)
    mid = rest.astype(BF16)
    return hi, mid, (rest - mid.astype(F32)).astype(BF16)


def kernel(
    n_seq, n_inner, kv, parts,
    q_hbm, k_hbm, v_hbm, ld_hbm, gain_hbm, list_hbm,
    out_ref,
    gain_ref, list_ref, qbuf, kbuf, vbuf, kx, vx, ldbuf, qs, kd, vd, vis, wmat, emat,
    score, prob, inv, lin, sp, state,
    local_sem, k_send, k_recv, v_send, v_recv, l_send, l_recv, x_send, x_recv,
    kx_send, kx_recv, vx_send, vx_recv,
):
    z = lax.axis_index("seq")
    x = lax.axis_index("inner")
    tokens, heads, width = qbuf.shape
    rep = heads // kv
    rows = tokens * rep
    pairs = tokens * kv
    per_piece = tokens // BLK
    keys_all = n_seq * tokens
    has_next, has_last = z < n_seq - 1, z > 0
    others = range(1, n_inner)

    barrier = pltpu.get_barrier_semaphore()

    ldbuf[...] = jnp.zeros_like(ldbuf)

    @pl.when(has_last)
    def _():
        pl.semaphore_signal(barrier, inc=1, device_id={"seq": z - 1}, device_id_type=MESH)

    for o in others:
        pl.semaphore_signal(
            barrier, inc=1, device_id={"inner": lax.rem(x + o, n_inner)}, device_id_type=MESH)

    q_copy = pltpu.make_async_copy(q_hbm, qbuf, local_sem.at[0])
    k_copy = pltpu.make_async_copy(k_hbm, kbuf.at[0], local_sem.at[1])
    v_copy = pltpu.make_async_copy(v_hbm, vbuf.at[0], local_sem.at[2])
    l_copy = pltpu.make_async_copy(ld_hbm, ldbuf.at[0, 0, 0:kv], local_sem.at[3])
    g_copy = pltpu.make_async_copy(gain_hbm, gain_ref, local_sem.at[4])
    list_copy = pltpu.make_async_copy(list_hbm, list_ref, local_sem.at[5])
    for copy in (l_copy, k_copy, v_copy, q_copy, list_copy, g_copy):
        copy.start()
    pl.semaphore_wait(barrier, n_inner - 1 + jnp.where(has_next, 1, 0))

    def hop(src, dst, send, recv):
        return pltpu.make_async_remote_copy(
            src_ref=src, dst_ref=dst, send_sem=send, recv_sem=recv,
            device_id={"seq": z + 1}, device_id_type=MESH)

    def across(o, src, dst, send, recv):
        return pltpu.make_async_remote_copy(
            src_ref=src, dst_ref=dst, send_sem=send, recv_sem=recv,
            device_id={"inner": lax.rem(x + o, n_inner)}, device_id_type=MESH)

    span = pairs // parts

    def part(ref, c):
        return ref.at[pl.ds(c * span, span)]

    def k_of(j):
        return k_hbm if j == 0 else kbuf.at[j]

    def v_of(j, c):
        return part(v_hbm if j == 0 else vbuf.at[j], c)

    def k_hop(j):
        return hop(k_of(j), kbuf.at[j + 1], k_send.at[j], k_recv.at[j + 1])

    def v_hop(j, c):
        return hop(v_of(j, c), part(vbuf.at[j + 1], c), v_send.at[j, c], v_recv.at[j + 1, c])

    def l_hop(j):
        return hop(
            ldbuf.at[j, :, 0:kv], ldbuf.at[j + 1, :, 0:kv], l_send.at[j], l_recv.at[j + 1])

    def k_across(o, j):
        s = n_inner - o
        return across(o, k_of(j), kx.at[s - 1, j], kx_send.at[o, j], kx_recv.at[s, j])

    def v_across(o, j, c):
        s = n_inner - o
        return across(
            o, v_of(j, c), part(vx.at[s - 1, j], c), vx_send.at[o, j, c], vx_recv.at[s, j, c])

    def x_copy(o):
        return across(o, ld_hbm, ldbuf.at[0, n_inner - o, 0:kv], x_send.at[o], x_recv.at[o])

    def relay(hops, j, spread=None):
        @pl.when(z >= j)
        def _():
            hops(j - 1).wait_recv()
            if spread is not None:
                for o in others:
                    spread(o, j).start()

        if j < n_seq - 1:

            @pl.when((z >= j) & has_next)
            def _():
                hops(j).start()

    def relay_k(j):
        relay(k_hop, j, k_across)

    def relay_v(j, c):
        relay(lambda i: v_hop(i, c), j, lambda o, i: v_across(o, i, c))

    @pl.when(has_next)
    def _():
        k_hop(0).start()
        for c in range(parts):
            v_hop(0, c).start()

    for o in others:
        x_copy(o).start()
    for o in others:
        k_across(o, 0).start()
        for c in range(parts):
            v_across(o, 0, c).start()

    for j in range(1, n_seq):

        @pl.when(z < j)
        def _():
            kbuf[j] = jnp.zeros_like(kbuf[j])
            vbuf[j] = jnp.zeros_like(vbuf[j])
            for o in others:
                kx[o - 1, j] = jnp.zeros_like(kx[o - 1, j])
                vx[o - 1, j] = jnp.zeros_like(vx[o - 1, j])

    state[...] = jnp.zeros_like(state)
    by_head = jnp.where(
        iota((pairs, pairs), 1) == lax.rem(iota((pairs, pairs), 0), tokens) * kv
        + iota((pairs, pairs), 0) // tokens, 1.0, 0.0
    ).astype(BF16)
    owner = lax.rem(iota((pairs, 1), 0), kv)
    after = jnp.where(
        iota((pairs, 2 * tokens), 1) > iota((pairs, 2 * tokens), 0) // kv, 1.0, 0.0
    ).astype(BF16)

    l_copy.wait()
    ld = ldbuf[0, 0]
    seen = iota((tokens, tokens), 0) >= iota((tokens, tokens), 1)
    upto = jnp.where(iota((tokens, tokens), 0) <= iota((tokens, tokens), 1), 1.0, 0.0)
    cum_lane = dot(ld, upto, precision=HIGH)
    ld_rows = jnp.concatenate(
        [jnp.broadcast_to(ld[g:g + 1, :], (width, tokens)) for g in range(kv)], axis=0)
    cum_all = dot(jnp.where(seen, 1.0, 0.0), ld_rows, ((1,), (1,)), HIGH)
    for g in range(kv):
        cum = cum_all[:, g * width:(g + 1) * width]
        emat[g] = jnp.exp(cum)
        wmat[g] = jnp.where(
            seen, jnp.exp(jnp.minimum(cum - cum_lane[g:g + 1, :], 0.0)), 0.0)

    def spread_rows(by_token):
        return jnp.broadcast_to(
            by_token[:, None, :], (tokens, rep, by_token.shape[1])
        ).reshape(rows, by_token.shape[1])

    def split(buf, dst, j):
        both = dot(by_head, buf[j]).astype(BF16)
        for g in range(kv):
            dst[g, j * tokens:(j + 1) * tokens, :] = both[g * tokens:(g + 1) * tokens]

    def absorb(k, v, ld_piece, later, valid=None):
        both = jnp.concatenate([ld_piece, later], axis=1)
        tail = sum(dot(after, t, ((1,), (1,))) for t in thirds(both))
        weight = jnp.exp(tail)
        if valid is not None:
            weight = jnp.where(valid, weight, 0.0)
        vf = v.astype(F32)
        weighted = jnp.concatenate(
            [vf * jnp.where(owner == g, weight[:, g:g + 1], 0.0) for g in range(kv)], axis=1)
        hi, lo = halves(weighted)
        state[...] += dot(
            jnp.concatenate([k, k], axis=0), jnp.concatenate([hi, lo], axis=0), ((0,), (0,)))

    def place(s):
        return lax.rem(x + s, n_inner)

    def between(j):
        total = jnp.zeros((LD_ROWS, tokens), F32)
        for s in others:
            total = total + jnp.where(place(s) < x, ldbuf[0, s], 0.0)
        for i in range(1, j):
            for s in range(n_inner):
                total = total + ldbuf[i, s]
        return total

    def absorb_row(j, s):
        if j == 0:
            later = jnp.zeros((LD_ROWS, tokens), F32)
            for r in others:
                later = later + jnp.where(
                    (place(r) > place(s)) & (place(r) < x), ldbuf[0, r], 0.0)
            absorb(kx[s - 1, 0], vx[s - 1, 0], ldbuf[0, s], later, place(s) < x)
            return
        later = between(j)
        for r in range(n_inner):
            if r != s:
                later = later + jnp.where(place(r) > place(s), ldbuf[j, r], 0.0)
        k, v = (kbuf[j], vbuf[j]) if s == 0 else (kx[s - 1, j], vx[s - 1, j])
        absorb(k, v, ldbuf[j, s], later)

    def absorb_others(j):
        for s in others:
            @pl.when(z >= j)
            def _():
                k_across(n_inner - s, j).wait_recv()
                for c in range(parts):
                    v_across(n_inner - s, j, c).wait_recv()
        for s in others:
            absorb_row(j, s)

    def visibility():
        list_copy.wait()
        lane = iota((1, keys_all), 1)
        key_block = (
            ((z - lane // tokens) * n_inner + x) * per_piece + lax.rem(lane, tokens) // BLK
        )
        listed = list_ref[...]
        for b in range(per_piece):
            member = key_block == listed[b:b + 1, 0:1]
            for i in range(1, listed.shape[1]):
                member = jnp.logical_or(member, key_block == listed[b:b + 1, i:i + 1])
            vis[b:b + 1, :] = jnp.where(member, 0.0, NEVER)

    def take_queries():
        q_copy.wait()
        qf = qbuf[...].astype(F32)
        for g in range(kv):
            qs[g] = qf[:, g * rep:(g + 1) * rep, :].reshape(rows, width).astype(BF16)

    half = BLK * rep

    def shown(s, j):
        cut = slice(j * tokens, (j + 1) * tokens)
        return jnp.concatenate(
            [s[b * half:(b + 1) * half] + vis[b:b + 1, cut] for b in range(per_piece)], axis=0)

    def own_piece(g):
        raw = dot(qs[g], kd[g, 0:tokens, :], ((1,), (1,)))
        past = iota((rows, tokens), 0) // rep >= iota((rows, tokens), 1)
        score[g, :, 0:tokens] = jnp.where(past, shown(raw, 0), NEVER)
        hi, lo = halves(raw * spread_rows(wmat[g]))
        v_g = vd[g, 0:tokens, :]
        lin[g] = dot(
            jnp.concatenate([hi, lo], axis=1), jnp.concatenate([v_g, v_g], axis=0))

    def score_piece(j):
        split(kbuf, kd, j)
        for g in range(kv):
            s = dot(qs[g], kd[g, j * tokens:(j + 1) * tokens, :], ((1,), (1,)))
            score[g, :, j * tokens:(j + 1) * tokens] = shown(s, j)

    scale = width ** (-0.5) * LOG2E

    def weigh(g, at):
        s = score[g, at, :]
        top = jnp.max(s, axis=1, keepdims=True)
        expo = jnp.exp2((s - top) * scale)
        denom = jnp.sum(expo, axis=1, keepdims=True)
        prob[g, at, :] = expo.astype(BF16)
        inv[g, at, :] = jnp.broadcast_to(1.0 / denom, (s.shape[0], width))

    k_copy.wait()
    v_copy.wait()
    split(kbuf, kd, 0)
    split(vbuf, vd, 0)
    for o in others:
        x_copy(o).wait_recv()

    @pl.when(has_next)
    def _():
        l_hop(0).start()

    take_queries()
    visibility()
    own_piece(0)

    weighing = [
        functools.partial(weigh, g, slice(b * half, (b + 1) * half))
        for g in range(kv) for b in range(per_piece)
    ]
    for j in range(1, n_seq):
        relay_k(j)
        if j == 1:
            for g in range(1, kv):
                own_piece(g)
        score_piece(j)
        last = j == n_seq - 1
        for c in range(parts):
            if last and weighing:
                weighing.pop(0)()
            relay_v(j, c)
        relay(l_hop, j)
        split(vbuf, vd, j)
        absorb_row(j, 0)
        absorb_others(j - 1)
    for item in weighing:
        item()
    for g in range(kv):
        sp[g] = dot(prob[g], vd[g]) * inv[g]
    g_copy.wait()
    absorb_others(n_seq - 1)

    done = []
    for g in range(kv):
        hi, lo = halves(state[:, g * width:(g + 1) * width])
        q_g = qs[g]
        inter = dot(
            jnp.concatenate([q_g, q_g], axis=1), jnp.concatenate([hi, lo], axis=0))
        linear = lin[g] + inter * spread_rows(emat[g])
        norm = lax.rsqrt(jnp.mean(linear * linear, axis=1, keepdims=True) + 1e-6)
        scaled = (linear * norm).reshape(tokens, rep, width) * gain_ref[g * rep:(g + 1) * rep, :][None]
        done.append(scaled + sp[g].reshape(tokens, rep, width))
    out_ref[...] = jnp.concatenate(done, axis=1).astype(out_ref.dtype)

    for j in range(n_seq - 1):

        @pl.when((z >= j) & has_next)
        def _():
            k_hop(j).wait_send()
            for c in range(parts):
                v_hop(j, c).wait_send()
            l_hop(j).wait_send()

    for o in others:
        x_copy(o).wait_send()
        for j in range(n_seq):

            @pl.when(z >= j)
            def _():
                k_across(o, j).wait_send()
                for c in range(parts):
                    v_across(o, j, c).wait_send()


def shards(n_seq, n_inner, queries, keys, values, log_decay, gain, block_list):
    tokens, heads, width = queries.shape
    kv = keys.shape[1]
    rows = tokens * (heads // kv)
    pairs = tokens * kv
    keys_all = n_seq * tokens
    parts = 4 if n_seq * n_inner <= 16 else 1
    side = max(n_inner - 1, 1)
    anywhere = pl.BlockSpec(memory_space=pl.ANY)
    dma = pltpu.SemaphoreType.DMA
    return pl.pallas_call(
        functools.partial(kernel, n_seq, n_inner, kv, parts),
        out_shape=pltpu.VMEM(queries.shape, queries.dtype),
        in_specs=[anywhere] * 6,
        out_specs=pl.BlockSpec(memory_space=pltpu.VMEM),
        scratch_shapes=[
            pltpu.VMEM(gain.shape, F32),
            pltpu.VMEM(block_list.shape, jnp.int32),
            pltpu.VMEM(queries.shape, BF16),
            pltpu.VMEM((n_seq, pairs, width), BF16),
            pltpu.VMEM((n_seq, pairs, width), BF16),
            pltpu.VMEM((side, n_seq, pairs, width), BF16),
            pltpu.VMEM((side, n_seq, pairs, width), BF16),
            pltpu.VMEM((n_seq, n_inner, LD_ROWS, tokens), F32),
            pltpu.VMEM((kv, rows, width), BF16),
            pltpu.VMEM((kv, keys_all, width), BF16),
            pltpu.VMEM((kv, keys_all, width), BF16),
            pltpu.VMEM((block_list.shape[0], keys_all), F32),
            pltpu.VMEM((kv, tokens, tokens), F32),
            pltpu.VMEM((kv, tokens, width), F32),
            pltpu.VMEM((kv, rows, keys_all), F32),
            pltpu.VMEM((kv, rows, keys_all), BF16),
            pltpu.VMEM((kv, rows, width), F32),
            pltpu.VMEM((kv, rows, width), F32),
            pltpu.VMEM((kv, rows, width), F32),
            pltpu.VMEM((width, kv * width), F32),
            dma((6,)),
            dma((n_seq,)), dma((n_seq,)), dma((n_seq, parts)), dma((n_seq, parts)),
            dma((n_seq,)), dma((n_seq,)), dma((n_inner,)), dma((n_inner,)),
            dma((n_inner, n_seq)), dma((n_inner, n_seq)),
            dma((n_inner, n_seq, parts)), dma((n_inner, n_seq, parts)),
        ],
        compiler_params=pltpu.CompilerParams(collective_id=0, has_side_effects=True),
        name="prefill",
    )(
        queries, keys.reshape(pairs, width), values.reshape(pairs, width),
        log_decay.T, gain, block_list,
    )


def solution(mesh):
    return jax.shard_map(
        functools.partial(shards, mesh.shape["seq"], mesh.shape["inner"]),
        mesh=mesh,
        in_specs=(
            P(("groups", "seq", "inner"), "head", None),
            P(("groups", "seq", "inner"), "head", None),
            P(("groups", "seq", "inner"), "head", None),
            P(("groups", "seq", "inner"), "head"),
            P("head", None),
            P(("groups", "seq", "inner"), None),
        ),
        out_specs=P(("groups", "seq", "inner"), "head", None),
        check_vma=False,
    )
```

```python
import functools

import jax
import jax.numpy as jnp
from jax import lax
from jax.experimental import pallas as pl
from jax.experimental.pallas import tpu as pltpu
from jax.sharding import PartitionSpec as P

BLK = 64
HIGH = lax.Precision.HIGHEST
MESH = pl.DeviceIdType.MESH
LD_ROWS = 8
F32 = jnp.float32
BF16 = jnp.bfloat16
LOG2E = 1.4426950408889634
NEVER = -1e30


def iota(shape, dim):
    return lax.broadcasted_iota(jnp.int32, shape, dim)


def dot(a, b, dims=((1,), (0,)), precision=None):
    return lax.dot_general(
        a, b, (dims, ((), ())), precision=precision, preferred_element_type=F32
    )


def halves(x):
    hi = x.astype(BF16)
    return hi, (x - hi.astype(F32)).astype(BF16)


def thirds(x):
    hi = x.astype(BF16)
    rest = x - hi.astype(F32)
    mid = rest.astype(BF16)
    return hi, mid, (rest - mid.astype(F32)).astype(BF16)


def kernel(
    n_seq, n_inner, kv, cuts,
    q_hbm, k_hbm, v_hbm, ld_hbm, gain_hbm, list_hbm,
    out_ref,
    gain_ref, list_ref, qbuf, raw, seg, cross, ldbuf, qs, vis, wmat, emat, cols,
    score, prob, inv, lin, sp, state,
    local_sem, k_recv, v_recv, h_send, l_send, l_recv, x_send, x_recv, c_send, c_recv,
):
    z = lax.axis_index("seq")
    x = lax.axis_index("inner")
    tokens, heads, width = qbuf.shape
    rep = heads // kv
    rows = tokens * rep
    pairs = tokens * kv
    per_piece = tokens // BLK
    keys_all = n_seq * tokens
    has_next, has_last = z < n_seq - 1, z > 0
    others = range(1, n_inner)
    last = n_seq - 1

    barrier = pltpu.get_barrier_semaphore()

    ldbuf[...] = jnp.zeros_like(ldbuf)

    @pl.when(has_last)
    def _():
        pl.semaphore_signal(barrier, inc=1, device_id={"seq": z - 1}, device_id_type=MESH)

    for o in others:
        pl.semaphore_signal(
            barrier, inc=1, device_id={"inner": lax.rem(x + o, n_inner)}, device_id_type=MESH)

    k_copy = pltpu.make_async_copy(k_hbm, raw.at[0], local_sem.at[1])
    v_copy = pltpu.make_async_copy(v_hbm, raw.at[1], local_sem.at[2])
    l_copy = pltpu.make_async_copy(ld_hbm, ldbuf.at[0, 0, 0:kv], local_sem.at[3])
    q_copy = pltpu.make_async_copy(q_hbm, qbuf, local_sem.at[0])
    g_copy = pltpu.make_async_copy(gain_hbm, gain_ref, local_sem.at[4])
    list_copy = pltpu.make_async_copy(list_hbm, list_ref, local_sem.at[5])
    for copy in (l_copy, k_copy, v_copy, q_copy, list_copy, g_copy):
        copy.start()

    by_head = jnp.where(
        iota((pairs, pairs), 1) == lax.rem(iota((pairs, pairs), 0), tokens) * kv
        + iota((pairs, pairs), 0) // tokens, 1.0, 0.0
    ).astype(BF16)
    l_copy.wait()
    k_copy.wait()
    v_copy.wait()
    apart = dot(by_head, jnp.concatenate([raw[0], raw[1]], axis=1)).astype(BF16)
    for i in range(2):
        for g in range(kv):
            seg[0, i, g] = apart[g * tokens:(g + 1) * tokens, i * width:(i + 1) * width]

    pl.semaphore_wait(barrier, n_inner - 1 + jnp.where(has_next, 1, 0))

    def hop(src, dst, send, recv):
        return pltpu.make_async_remote_copy(
            src_ref=src, dst_ref=dst, send_sem=send, recv_sem=recv,
            device_id={"seq": z + 1}, device_id_type=MESH)

    def across(o, src, dst, send, recv):
        return pltpu.make_async_remote_copy(
            src_ref=src, dst_ref=dst, send_sem=send, recv_sem=recv,
            device_id={"inner": lax.rem(x + o, n_inner)}, device_id_type=MESH)

    def part(ref, i, c):
        per_head = cuts[i] // kv
        if per_head == 0:
            return ref.at[i]
        span = tokens // per_head
        return ref.at[i, c // per_head, pl.ds(c % per_head * span, span)]

    def part_hop(j, i, c):
        return hop(
            part(seg.at[j], i, c), part(seg.at[j + 1], i, c), h_send.at[j],
            (k_recv, v_recv)[i].at[j + 1, c])

    def piece_hop(j):
        return hop(seg.at[j], seg.at[j + 1], h_send.at[j], k_recv.at[j + 1, 0])

    def l_hop(j):
        return hop(
            ldbuf.at[j, 0, 0:kv], ldbuf.at[j + 1, 0, 0:kv], l_send.at[j], l_recv.at[j + 1])

    def part_across(o, j, i, c):
        s = n_inner - o
        return across(
            o, part(seg.at[j], i, c), part(cross.at[s - 1, j], i, c), c_send.at[o, j],
            c_recv.at[s, j])

    def piece_across(o, j):
        s = n_inner - o
        return across(o, seg.at[j], cross.at[s - 1, j], c_send.at[o, j], c_recv.at[s, j])

    def l_across(o, j):
        s = n_inner - o
        return across(
            o, ldbuf.at[j, 0, 0:kv], ldbuf.at[j, s, 0:kv], x_send.at[o, j], x_recv.at[s, j])

    def relay_part(j, i, c):
        @pl.when(z >= j)
        def _():
            part_hop(j - 1, i, c).wait_recv()
            if j < last:

                @pl.when(has_next)
                def _():
                    part_hop(j, i, c).start()

            for o in others:
                part_across(o, j, i, c).start()

    def relay_l(j):
        @pl.when(z >= j)
        def _():
            l_hop(j - 1).wait_recv()
            if j < last:

                @pl.when(has_next)
                def _():
                    l_hop(j).start()

            for o in others:
                l_across(o, j).start()

    @pl.when(has_next)
    def _():
        l_hop(0).start()
        for i in range(2):
            for c in range(cuts[i]):
                part_hop(0, i, c).start()

    for o in others:
        l_across(o, 0).start()

        @pl.when(x + o < n_inner)
        def _():
            piece_across(o, 0).start()

    for s in others:

        @pl.when(x + s < n_inner)
        def _():
            cross[s - 1, 0] = jnp.zeros_like(cross[s - 1, 0])

    for j in range(1, n_seq):

        @pl.when(z < j)
        def _():
            seg[j] = jnp.zeros_like(seg[j])
            for o in others:
                cross[o - 1, j] = jnp.zeros_like(cross[o - 1, j])

    def spread_rows(by_token):
        return jnp.broadcast_to(
            by_token[:, None, :], (tokens, rep, by_token.shape[1])
        ).reshape(rows, by_token.shape[1])

    state[...] = jnp.zeros_like(state)
    after = jnp.where(
        iota((tokens, 2 * tokens), 1) > iota((tokens, 2 * tokens), 0), 1.0, 0.0
    ).astype(BF16)

    def decays():
        ld = ldbuf[0, 0]
        seen = iota((tokens, tokens), 0) >= iota((tokens, tokens), 1)
        upto = jnp.where(iota((tokens, tokens), 0) <= iota((tokens, tokens), 1), 1.0, 0.0)
        cum_lane = dot(ld, upto, precision=HIGH)
        ld_rows = jnp.concatenate(
            [jnp.broadcast_to(ld[g:g + 1, :], (width, tokens)) for g in range(kv)], axis=0)
        cum_all = dot(jnp.where(seen, 1.0, 0.0), ld_rows, ((1,), (1,)), HIGH)
        for g in range(kv):
            cum = cum_all[:, g * width:(g + 1) * width]
            emat[g] = spread_rows(jnp.exp(cum))
            wmat[g] = jnp.where(
                seen, jnp.exp(jnp.minimum(cum - cum_lane[g:g + 1, :], 0.0)), 0.0)

    def place(s):
        return lax.rem(x + s, n_inner)

    def later_than(j, s):
        total = jnp.zeros((LD_ROWS, tokens), F32)
        for r in range(n_inner):
            if j == 0 and r > 0:
                total = total + jnp.where(
                    (place(r) > place(s)) & (place(r) < x), ldbuf[0, r], 0.0)
            elif j > 0:
                if r != s:
                    total = total + jnp.where(place(r) > place(s), ldbuf[j, r], 0.0)
                if r > 0:
                    total = total + jnp.where(place(r) < x, ldbuf[0, r], 0.0)
                for i in range(1, j):
                    total = total + ldbuf[i, r]
        return total

    def weigh_pieces(pieces):
        both = jnp.concatenate([
            jnp.concatenate([ldbuf[j, s], later_than(j, s)], axis=1) for j, s in pieces], axis=0)
        tail = dot(
            jnp.concatenate([after] * 3, axis=1), jnp.concatenate(thirds(both), axis=1),
            ((1,), (1,)))
        weight = jnp.exp(tail)
        for n, (j, s) in enumerate(pieces):
            for g in range(kv):
                col = weight[:, n * LD_ROWS + g:n * LD_ROWS + g + 1]
                if j == 0:
                    col = jnp.where(place(s) < x, col, 0.0)
                cols[j % 3, s, g] = jnp.broadcast_to(col, (tokens, width))

    def absorb(pieces):
        for g in range(kv):
            left, right = [], []
            for j, s in pieces:
                piece = seg.at[j] if s == 0 else cross.at[s - 1, j]
                k_g = piece[0, g]
                hi, lo = halves(piece[1, g].astype(F32) * cols[j % 3, s, g])
                left += [k_g, k_g]
                right += [hi, lo]
            state[g] += dot(
                jnp.concatenate(left, axis=0), jnp.concatenate(right, axis=0), ((0,), (0,)))

    def row_of(j):
        return [(j, s) for s in range(1 if j == 0 else 0, n_inner)]

    def arrive_l(j):
        for s in others:

            @pl.when(z >= j)
            def _():
                l_across(n_inner - s, j).wait_recv()

    def arrive(j):
        for s in others:
            @pl.when((x + s >= n_inner) if j == 0 else (z >= j))
            def _():
                piece_across(n_inner - s, j).wait_recv()


    def visibility():
        list_copy.wait()
        lane = iota((1, keys_all), 1)
        key_block = (
            ((z - lane // tokens) * n_inner + x) * per_piece + lax.rem(lane, tokens) // BLK
        )
        listed = list_ref[...]
        for b in range(per_piece):
            member = key_block == listed[b:b + 1, 0:1]
            for i in range(1, listed.shape[1]):
                member = jnp.logical_or(member, key_block == listed[b:b + 1, i:i + 1])
            vis[b:b + 1, :] = jnp.where(member, 0.0, NEVER)

    def take_queries():
        q_copy.wait()
        qf = qbuf[...].astype(F32)
        for g in range(kv):
            qs[g] = qf[:, g * rep:(g + 1) * rep, :].reshape(rows, width).astype(BF16)

    half = BLK * rep
    scale = width ** (-0.5) * LOG2E

    def shown(s, j):
        cut = slice(j * tokens, (j + 1) * tokens)
        return jnp.concatenate(
            [s[b * half:(b + 1) * half] * scale + vis[b:b + 1, cut] for b in range(per_piece)],
            axis=0)

    def own_piece(g):
        plain = dot(qs[g], seg[0, 0, g], ((1,), (1,)))
        past = iota((rows, tokens), 0) // rep >= iota((rows, tokens), 1)
        score[g, :, 0:tokens] = jnp.where(past, shown(plain, 0), NEVER)
        hi, lo = halves(plain * spread_rows(wmat[g]))
        v_g = seg[0, 1, g]
        lin[g] = dot(
            jnp.concatenate([hi, lo], axis=1), jnp.concatenate([v_g, v_g], axis=0))

    def score_piece(j):
        for g in range(kv):
            s = dot(qs[g], seg[j, 0, g], ((1,), (1,)))
            score[g, :, j * tokens:(j + 1) * tokens] = shown(s, j)

    def weigh(g, at):
        s = score[g, at, :]
        top = jnp.max(s, axis=1, keepdims=True)
        expo = jnp.exp2(s - top)
        denom = jnp.sum(expo, axis=1, keepdims=True)
        prob[g, at, :] = expo.astype(BF16)
        inv[g, at, :] = jnp.broadcast_to(1.0 / denom, (s.shape[0], width))

    def sparse(g):
        v_g = jnp.concatenate([seg[j, 1, g] for j in range(n_seq)], axis=0)
        sp[g] = dot(prob[g], v_g) * inv[g]

    decays()
    take_queries()
    visibility()
    for g in range(kv):
        own_piece(g)

    weighing = [
        functools.partial(weigh, g, slice(b * half, (b + 1) * half))
        for g in range(kv) for b in range(per_piece)
    ]
    for j in range(1, n_seq):
        relay_l(j)
        for c in range(cuts[0]):
            relay_part(j, 0, c)
        arrive_l(j - 1)
        score_piece(j)
        weigh_pieces(row_of(j - 1))
        for c in range(cuts[1]):
            relay_part(j, 1, c)
            if j == last and weighing:
                weighing.pop(0)()
        if j > 1:
            arrive(j - 2)
            absorb(row_of(j - 2))
    for item in weighing:
        item()
    for g in range(kv):
        sparse(g)
    if n_seq > 1:
        arrive(last - 1)
        absorb(row_of(last - 1))
    g_copy.wait()
    gains = gain_ref[...] * width ** 0.5

    for j in range(last):

        @pl.when((z >= j) & has_next)
        def _():
            piece_hop(j).wait_send()
            l_hop(j).wait_send()

    for o in others:
        for j in range(last):

            @pl.when(z >= j)
            def _():
                l_across(o, j).wait_send()

            @pl.when((x + o < n_inner) if j == 0 else (z >= j))
            def _():
                piece_across(o, j).wait_send()

    arrive_l(last)
    weigh_pieces(row_of(last))
    arrive(last)
    absorb(row_of(last))

    done = []
    for g in range(kv):
        hi, lo = halves(state[g])
        q_g = qs[g]
        inter = dot(
            jnp.concatenate([q_g, q_g], axis=1), jnp.concatenate([hi, lo], axis=0))
        linear = lin[g] + inter * emat[g]
        norm = lax.rsqrt(jnp.sum(linear * linear, axis=1, keepdims=True) + width * 1e-6)
        scaled = (linear * norm).reshape(tokens, rep, width) * gains[g * rep:(g + 1) * rep, :][None]
        done.append(scaled + sp[g].reshape(tokens, rep, width))
    out_ref[...] = jnp.concatenate(done, axis=1).astype(out_ref.dtype)

    for o in others:

        @pl.when(z >= last)
        def _():
            l_across(o, last).wait_send()
            piece_across(o, last).wait_send()


def shards(n_seq, n_inner, queries, keys, values, log_decay, gain, block_list):
    tokens, heads, width = queries.shape
    kv = keys.shape[1]
    rows = tokens * (heads // kv)
    pairs = tokens * kv
    keys_all = n_seq * tokens
    cuts = (kv, 2 * kv) if n_seq * n_inner <= 16 else (1, 1)
    side = max(n_inner - 1, 1)
    anywhere = pl.BlockSpec(memory_space=pl.ANY)
    dma = pltpu.SemaphoreType.DMA
    return pl.pallas_call(
        functools.partial(kernel, n_seq, n_inner, kv, cuts),
        out_shape=pltpu.VMEM(queries.shape, queries.dtype),
        in_specs=[anywhere] * 6,
        out_specs=pl.BlockSpec(memory_space=pltpu.VMEM),
        scratch_shapes=[
            pltpu.VMEM(gain.shape, F32),
            pltpu.VMEM(block_list.shape, jnp.int32),
            pltpu.VMEM(queries.shape, BF16),
            pltpu.VMEM((2, pairs, width), BF16),
            pltpu.VMEM((n_seq, 2, kv, tokens, width), BF16),
            pltpu.VMEM((side, n_seq, 2, kv, tokens, width), BF16),
            pltpu.VMEM((n_seq, n_inner, LD_ROWS, tokens), F32),
            pltpu.VMEM((kv, rows, width), BF16),
            pltpu.VMEM((block_list.shape[0], keys_all), F32),
            pltpu.VMEM((kv, tokens, tokens), F32),
            pltpu.VMEM((kv, rows, width), F32),
            pltpu.VMEM((3, n_inner, kv, tokens, width), F32),
            pltpu.VMEM((kv, rows, keys_all), F32),
            pltpu.VMEM((kv, rows, keys_all), BF16),
            pltpu.VMEM((kv, rows, width), F32),
            pltpu.VMEM((kv, rows, width), F32),
            pltpu.VMEM((kv, rows, width), F32),
            pltpu.VMEM((kv, width, width), F32),
            dma((6,)),
            dma((n_seq, cuts[0])), dma((n_seq, cuts[1])), dma((n_seq,)),
            dma((n_seq,)), dma((n_seq,)), dma((n_inner, n_seq)), dma((n_inner, n_seq)),
            dma((n_inner, n_seq)), dma((n_inner, n_seq)),
        ],
        compiler_params=pltpu.CompilerParams(collective_id=0, has_side_effects=True),
        name="prefill",
    )(
        queries, keys.reshape(pairs, width), values.reshape(pairs, width),
        log_decay.T, gain, block_list,
    )


def solution(mesh):
    return jax.shard_map(
        functools.partial(shards, mesh.shape["seq"], mesh.shape["inner"]),
        mesh=mesh,
        in_specs=(
            P(("groups", "seq", "inner"), "head", None),
            P(("groups", "seq", "inner"), "head", None),
            P(("groups", "seq", "inner"), "head", None),
            P(("groups", "seq", "inner"), "head"),
            P("head", None),
            P(("groups", "seq", "inner"), None),
        ),
        out_specs=P(("groups", "seq", "inner"), "head", None),
        check_vma=False,
    )
```

```python
import functools

import jax
import jax.numpy as jnp
from jax import lax
from jax.experimental import pallas as pl
from jax.experimental.pallas import tpu as pltpu
from jax.sharding import PartitionSpec as P

BLK = 64
HIGH = lax.Precision.HIGHEST
MESH = pl.DeviceIdType.MESH
LD_ROWS = 8
F32 = jnp.float32
BF16 = jnp.bfloat16
LOG2E = 1.4426950408889634
NEVER = -1e30


def iota(shape, dim):
    return lax.broadcasted_iota(jnp.int32, shape, dim)


def dot(a, b, dims=((1,), (0,)), precision=None):
    return lax.dot_general(
        a, b, (dims, ((), ())), precision=precision, preferred_element_type=F32
    )


def halves(x):
    hi = x.astype(BF16)
    return hi, (x - hi.astype(F32)).astype(BF16)


def thirds(x):
    hi = x.astype(BF16)
    rest = x - hi.astype(F32)
    mid = rest.astype(BF16)
    return hi, mid, (rest - mid.astype(F32)).astype(BF16)


def kernel(
    n_seq, n_inner, kv, cuts,
    q_hbm, k_hbm, v_hbm, ld_hbm, gain_hbm, list_hbm,
    out_ref,
    gain_ref, list_ref, qbuf, raw, seg, cross, ldbuf, qs, vis, wmat, emat, cols,
    score, prob, inv, lin, sp, state,
    local_sem, k_recv, v_recv, h_send, l_send, l_recv, x_send, x_recv, c_send, c_recv,
):
    z = lax.axis_index("seq")
    x = lax.axis_index("inner")
    tokens, heads, width = qbuf.shape
    rep = heads // kv
    rows = tokens * rep
    pairs = tokens * kv
    per_piece = tokens // BLK
    keys_all = n_seq * tokens
    has_next, has_last = z < n_seq - 1, z > 0
    others = range(1, n_inner)
    last = n_seq - 1

    barrier = pltpu.get_barrier_semaphore()

    ldbuf[...] = jnp.zeros_like(ldbuf)

    @pl.when(has_last)
    def _():
        pl.semaphore_signal(barrier, inc=1, device_id={"seq": z - 1}, device_id_type=MESH)

    for o in others:
        pl.semaphore_signal(
            barrier, inc=1, device_id={"inner": lax.rem(x + o, n_inner)}, device_id_type=MESH)

    k_copy = pltpu.make_async_copy(k_hbm, raw.at[0], local_sem.at[1])
    v_copy = pltpu.make_async_copy(v_hbm, raw.at[1], local_sem.at[2])
    l_copy = pltpu.make_async_copy(ld_hbm, ldbuf.at[0, 0, 0:kv], local_sem.at[3])
    q_copy = pltpu.make_async_copy(q_hbm, qbuf, local_sem.at[0])
    g_copy = pltpu.make_async_copy(gain_hbm, gain_ref, local_sem.at[4])
    list_copy = pltpu.make_async_copy(list_hbm, list_ref, local_sem.at[5])
    for copy in (l_copy, k_copy, v_copy, q_copy, list_copy, g_copy):
        copy.start()

    by_head = jnp.where(
        iota((pairs, pairs), 1) == lax.rem(iota((pairs, pairs), 0), tokens) * kv
        + iota((pairs, pairs), 0) // tokens, 1.0, 0.0
    ).astype(BF16)
    l_copy.wait()
    k_copy.wait()
    v_copy.wait()
    apart = dot(by_head, jnp.concatenate([raw[0], raw[1]], axis=1)).astype(BF16)
    for i in range(2):
        for g in range(kv):
            seg[0, i, g] = apart[g * tokens:(g + 1) * tokens, i * width:(i + 1) * width]

    pl.semaphore_wait(barrier, n_inner - 1 + jnp.where(has_next, 1, 0))

    def hop(src, dst, send, recv):
        return pltpu.make_async_remote_copy(
            src_ref=src, dst_ref=dst, send_sem=send, recv_sem=recv,
            device_id={"seq": z + 1}, device_id_type=MESH)

    def across(o, src, dst, send, recv):
        return pltpu.make_async_remote_copy(
            src_ref=src, dst_ref=dst, send_sem=send, recv_sem=recv,
            device_id={"inner": lax.rem(x + o, n_inner)}, device_id_type=MESH)

    def part(ref, i, c):
        per_head = cuts[i] // kv
        if per_head == 0:
            return ref.at[i]
        span = tokens // per_head
        return ref.at[i, c // per_head, pl.ds(c % per_head * span, span)]

    def part_hop(j, i, c):
        return hop(
            part(seg.at[j], i, c), part(seg.at[j + 1], i, c), h_send.at[j],
            (k_recv, v_recv)[i].at[j, c])

    def piece_hop(j):
        return hop(seg.at[j], seg.at[j + 1], h_send.at[j], k_recv.at[j, 0])

    def l_hop(j):
        return hop(
            ldbuf.at[j, 0, 0:kv], ldbuf.at[j + 1, 0, 0:kv], l_send.at[j], l_recv.at[j])

    def part_across(o, j, i, c):
        s = n_inner - o
        return across(
            o, part(seg.at[j], i, c), part(cross.at[s - 1, j], i, c), c_send.at[o - 1, j],
            c_recv.at[s - 1, j])

    def piece_across(o, j):
        s = n_inner - o
        return across(o, seg.at[j], cross.at[s - 1, j], c_send.at[o - 1, j], c_recv.at[s - 1, j])

    def l_across(o, j):
        s = n_inner - o
        return across(
            o, ldbuf.at[j, 0, 0:kv], ldbuf.at[j, s, 0:kv], x_send.at[o - 1, j], x_recv.at[s - 1, j])

    def relay_part(j, i, c):
        @pl.when(z >= j)
        def _():
            part_hop(j - 1, i, c).wait_recv()
            if j < last:

                @pl.when(has_next)
                def _():
                    part_hop(j, i, c).start()

            for o in others:
                part_across(o, j, i, c).start()

    def relay_l(j):
        @pl.when(z >= j)
        def _():
            l_hop(j - 1).wait_recv()
            if j < last:

                @pl.when(has_next)
                def _():
                    l_hop(j).start()

            for o in others:
                l_across(o, j).start()

    @pl.when(has_next)
    def _():
        l_hop(0).start()
        for i in range(2):
            for c in range(cuts[i]):
                part_hop(0, i, c).start()

    for o in others:
        l_across(o, 0).start()

        @pl.when(x + o < n_inner)
        def _():
            piece_across(o, 0).start()

    for s in others:

        @pl.when(x + s < n_inner)
        def _():
            cross[s - 1, 0] = jnp.zeros_like(cross[s - 1, 0])

    for j in range(1, n_seq):

        @pl.when(z < j)
        def _():
            seg[j] = jnp.zeros_like(seg[j])
            for o in others:
                cross[o - 1, j] = jnp.zeros_like(cross[o - 1, j])

    def spread_rows(by_token):
        return jnp.broadcast_to(
            by_token[:, None, :], (tokens, rep, by_token.shape[1])
        ).reshape(rows, by_token.shape[1])

    state[...] = jnp.zeros_like(state)
    after = jnp.where(
        iota((tokens, 2 * tokens), 1) > iota((tokens, 2 * tokens), 0), 1.0, 0.0
    ).astype(BF16)

    def decays():
        ld = ldbuf[0, 0]
        seen = iota((tokens, tokens), 0) >= iota((tokens, tokens), 1)
        upto = jnp.where(iota((tokens, tokens), 0) <= iota((tokens, tokens), 1), 1.0, 0.0)
        cum_lane = dot(ld, upto, precision=HIGH)
        ld_rows = jnp.concatenate(
            [jnp.broadcast_to(ld[g:g + 1, :], (width, tokens)) for g in range(kv)], axis=0)
        cum_all = dot(jnp.where(seen, 1.0, 0.0), ld_rows, ((1,), (1,)), HIGH)
        for g in range(kv):
            cum = cum_all[:, g * width:(g + 1) * width]
            emat[g] = spread_rows(jnp.exp(cum))
            wmat[g] = jnp.where(
                seen, jnp.exp(jnp.minimum(cum - cum_lane[g:g + 1, :], 0.0)), 0.0)

    def place(s):
        return lax.rem(x + s, n_inner)

    def later_than(j, s):
        total = jnp.zeros((LD_ROWS, tokens), F32)
        for r in range(n_inner):
            if j == 0 and r > 0:
                total = total + jnp.where(
                    (place(r) > place(s)) & (place(r) < x), ldbuf[0, r], 0.0)
            elif j > 0:
                if r != s:
                    total = total + jnp.where(place(r) > place(s), ldbuf[j, r], 0.0)
                if r > 0:
                    total = total + jnp.where(place(r) < x, ldbuf[0, r], 0.0)
                for i in range(1, j):
                    total = total + ldbuf[i, r]
        return total

    def weigh_pieces(pieces):
        both = jnp.concatenate([
            jnp.concatenate([ldbuf[j, s], later_than(j, s)], axis=1) for j, s in pieces], axis=0)
        tail = dot(
            jnp.concatenate([after] * 3, axis=1), jnp.concatenate(thirds(both), axis=1),
            ((1,), (1,)))
        weight = jnp.exp(tail)
        for n, (j, s) in enumerate(pieces):
            for g in range(kv):
                col = weight[:, n * LD_ROWS + g:n * LD_ROWS + g + 1]
                if j == 0:
                    col = jnp.where(place(s) < x, col, 0.0)
                cols[j % 3, s, g] = jnp.broadcast_to(col, (tokens, width))

    def absorb(pieces):
        for g in range(kv):
            left, right = [], []
            for j, s in pieces:
                piece = seg.at[j] if s == 0 else cross.at[s - 1, j]
                k_g = piece[0, g]
                hi, lo = halves(piece[1, g].astype(F32) * cols[j % 3, s, g])
                left += [k_g, k_g]
                right += [hi, lo]
            state[g] += dot(
                jnp.concatenate(left, axis=0), jnp.concatenate(right, axis=0), ((0,), (0,)))

    def row_of(j):
        return [(j, s) for s in range(1 if j == 0 else 0, n_inner)]

    def arrive_l(j):
        for s in others:

            @pl.when(z >= j)
            def _():
                l_across(n_inner - s, j).wait_recv()

    def arrive(j):
        for s in others:
            @pl.when((x + s >= n_inner) if j == 0 else (z >= j))
            def _():
                piece_across(n_inner - s, j).wait_recv()


    def visibility():
        list_copy.wait()
        lane = iota((1, keys_all), 1)
        key_block = (
            ((z - lane // tokens) * n_inner + x) * per_piece + lax.rem(lane, tokens) // BLK
        )
        listed = list_ref[...]
        for b in range(per_piece):
            member = key_block == listed[b:b + 1, 0:1]
            for i in range(1, listed.shape[1]):
                member = jnp.logical_or(member, key_block == listed[b:b + 1, i:i + 1])
            vis[b:b + 1, :] = jnp.where(member, 0.0, NEVER)

    def take_queries():
        q_copy.wait()
        qf = qbuf[...].astype(F32)
        for g in range(kv):
            qs[g] = qf[:, g * rep:(g + 1) * rep, :].reshape(rows, width).astype(BF16)

    half = BLK * rep
    scale = width ** (-0.5) * LOG2E

    def shown(s, j):
        cut = slice(j * tokens, (j + 1) * tokens)
        return jnp.concatenate(
            [s[b * half:(b + 1) * half] * scale + vis[b:b + 1, cut] for b in range(per_piece)],
            axis=0)

    def own_piece(g):
        plain = dot(qs[g], seg[0, 0, g], ((1,), (1,)))
        past = iota((rows, tokens), 0) // rep >= iota((rows, tokens), 1)
        score[g, :, 0:tokens] = jnp.where(past, shown(plain, 0), NEVER)
        hi, lo = halves(plain * spread_rows(wmat[g]))
        v_g = seg[0, 1, g]
        lin[g] = dot(
            jnp.concatenate([hi, lo], axis=1), jnp.concatenate([v_g, v_g], axis=0))

    def score_piece(j):
        for g in range(kv):
            s = dot(qs[g], seg[j, 0, g], ((1,), (1,)))
            score[g, :, j * tokens:(j + 1) * tokens] = shown(s, j)

    def weigh(g, at):
        s = score[g, at, :]
        top = jnp.max(s, axis=1, keepdims=True)
        expo = jnp.exp2(s - top)
        denom = jnp.sum(expo, axis=1, keepdims=True)
        prob[g, at, :] = expo.astype(BF16)
        inv[g, at, :] = jnp.broadcast_to(1.0 / denom, (s.shape[0], width))

    def sparse(g):
        v_g = jnp.concatenate([seg[j, 1, g] for j in range(n_seq)], axis=0)
        sp[g] = dot(prob[g], v_g) * inv[g]

    decays()
    take_queries()
    visibility()
    for g in range(kv):
        own_piece(g)

    weighing = [
        functools.partial(weigh, g, slice(b * half, (b + 1) * half))
        for g in range(kv) for b in range(per_piece)
    ]
    for j in range(1, n_seq):
        relay_l(j)
        for c in range(cuts[0]):
            relay_part(j, 0, c)
        arrive_l(j - 1)
        score_piece(j)
        weigh_pieces(row_of(j - 1))
        for c in range(cuts[1]):
            relay_part(j, 1, c)
        if j == last:
            for item in weighing:
                item()
        if j > 1:
            arrive(j - 2)
            absorb(row_of(j - 2))
    if n_seq == 1:
        for item in weighing:
            item()
    for g in range(kv):
        sparse(g)
    arrive_l(last)
    weigh_pieces(row_of(last))
    if n_seq > 1:
        arrive(last - 1)
        absorb(row_of(last - 1) + [(last, 0)])
    g_copy.wait()
    gains = gain_ref[...] * width ** 0.5

    for j in range(last):

        @pl.when((z >= j) & has_next)
        def _():
            piece_hop(j).wait_send()
            l_hop(j).wait_send()

    for o in others:
        for j in range(last):

            @pl.when(z >= j)
            def _():
                l_across(o, j).wait_send()

            @pl.when((x + o < n_inner) if j == 0 else (z >= j))
            def _():
                piece_across(o, j).wait_send()

    arrive(last)
    absorb([(last, s) for s in others])

    done = []
    for g in range(kv):
        hi, lo = halves(state[g])
        q_g = qs[g]
        inter = dot(
            jnp.concatenate([q_g, q_g], axis=1), jnp.concatenate([hi, lo], axis=0))
        linear = lin[g] + inter * emat[g]
        norm = lax.rsqrt(jnp.sum(linear * linear, axis=1, keepdims=True) + width * 1e-6)
        scaled = (linear * norm).reshape(tokens, rep, width) * gains[g * rep:(g + 1) * rep, :][None]
        done.append(scaled + sp[g].reshape(tokens, rep, width))
    out_ref[...] = jnp.concatenate(done, axis=1).astype(out_ref.dtype)

    for o in others:

        @pl.when(z >= last)
        def _():
            l_across(o, last).wait_send()
            piece_across(o, last).wait_send()


def shards(n_seq, n_inner, queries, keys, values, log_decay, gain, block_list):
    tokens, heads, width = queries.shape
    kv = keys.shape[1]
    rows = tokens * (heads // kv)
    pairs = tokens * kv
    keys_all = n_seq * tokens
    cuts = (kv, 2 * kv) if n_seq * n_inner <= 16 else (1, 1)
    side, hops = max(n_inner - 1, 1), max(n_seq - 1, 1)
    anywhere = pl.BlockSpec(memory_space=pl.ANY)
    dma = pltpu.SemaphoreType.DMA
    return pl.pallas_call(
        functools.partial(kernel, n_seq, n_inner, kv, cuts),
        out_shape=pltpu.VMEM(queries.shape, queries.dtype),
        in_specs=[anywhere] * 6,
        out_specs=pl.BlockSpec(memory_space=pltpu.VMEM),
        scratch_shapes=[
            pltpu.VMEM(gain.shape, F32),
            pltpu.VMEM(block_list.shape, jnp.int32),
            pltpu.VMEM(queries.shape, BF16),
            pltpu.VMEM((2, pairs, width), BF16),
            pltpu.VMEM((n_seq, 2, kv, tokens, width), BF16),
            pltpu.VMEM((side, n_seq, 2, kv, tokens, width), BF16),
            pltpu.VMEM((n_seq, n_inner, LD_ROWS, tokens), F32),
            pltpu.VMEM((kv, rows, width), BF16),
            pltpu.VMEM((block_list.shape[0], keys_all), F32),
            pltpu.VMEM((kv, tokens, tokens), F32),
            pltpu.VMEM((kv, rows, width), F32),
            pltpu.VMEM((3, n_inner, kv, tokens, width), F32),
            pltpu.VMEM((kv, rows, keys_all), F32),
            pltpu.VMEM((kv, rows, keys_all), BF16),
            pltpu.VMEM((kv, rows, width), F32),
            pltpu.VMEM((kv, rows, width), F32),
            pltpu.VMEM((kv, rows, width), F32),
            pltpu.VMEM((kv, width, width), F32),
            dma((6,)),
            dma((hops, cuts[0])), dma((hops, cuts[1])), dma((hops,)),
            dma((hops,)), dma((hops,)), dma((side, n_seq)), dma((side, n_seq)),
            dma((side, n_seq)), dma((side, n_seq)),
        ],
        compiler_params=pltpu.CompilerParams(collective_id=0, has_side_effects=True),
        name="prefill",
    )(
        queries, keys.reshape(pairs, width), values.reshape(pairs, width),
        log_decay.T, gain, block_list,
    )


def solution(mesh):
    return jax.shard_map(
        functools.partial(shards, mesh.shape["seq"], mesh.shape["inner"]),
        mesh=mesh,
        in_specs=(
            P(("groups", "seq", "inner"), "head", None),
            P(("groups", "seq", "inner"), "head", None),
            P(("groups", "seq", "inner"), "head", None),
            P(("groups", "seq", "inner"), "head"),
            P("head", None),
            P(("groups", "seq", "inner"), None),
        ),
        out_specs=P(("groups", "seq", "inner"), "head", None),
        check_vma=False,
    )
```

```python
import functools

import jax
import jax.numpy as jnp
from jax import lax
from jax.experimental import pallas as pl
from jax.experimental.pallas import tpu as pltpu
from jax.sharding import PartitionSpec as P

BLK = 64
HIGH = lax.Precision.HIGHEST
MESH = pl.DeviceIdType.MESH
LD_ROWS = 8
F32 = jnp.float32
BF16 = jnp.bfloat16
LOG2E = 1.4426950408889634
NEVER = -1e30


def iota(shape, dim):
    return lax.broadcasted_iota(jnp.int32, shape, dim)


def dot(a, b, dims=((1,), (0,)), precision=None):
    return lax.dot_general(
        a, b, (dims, ((), ())), precision=precision, preferred_element_type=F32
    )


def halves(x):
    hi = x.astype(BF16)
    return hi, (x - hi.astype(F32)).astype(BF16)


def thirds(x):
    hi = x.astype(BF16)
    rest = x - hi.astype(F32)
    mid = rest.astype(BF16)
    return hi, mid, (rest - mid.astype(F32)).astype(BF16)


def kernel(
    n_seq, n_inner, kv, cuts,
    q_hbm, k_hbm, v_hbm, ld_hbm, gain_hbm, list_hbm,
    out_ref,
    gain_ref, list_ref, qbuf, raw, seg, cross, ldbuf, qs, vis, wmat, emat, cols,
    score, prob, inv, lin, sp, state,
    local_sem, k_recv, v_recv, h_send, l_send, l_recv, x_send, x_recv, c_send, c_recv,
    a_send, a_recv,
):
    z = lax.axis_index("seq")
    x = lax.axis_index("inner")
    tokens, heads, width = qbuf.shape
    rep = heads // kv
    rows = tokens * rep
    pairs = tokens * kv
    per_piece = tokens // BLK
    keys_all = n_seq * tokens
    has_next, has_last = z < n_seq - 1, z > 0
    others = range(1, n_inner)
    last = n_seq - 1
    around = last > 1
    first = lax.axis_index("head") == 0

    barrier = pltpu.get_barrier_semaphore()

    ldbuf[...] = jnp.zeros_like(ldbuf)

    @pl.when(has_last)
    def _():
        pl.semaphore_signal(barrier, inc=1, device_id={"seq": z - 1}, device_id_type=MESH)

    for o in others:
        pl.semaphore_signal(
            barrier, inc=1, device_id={"inner": lax.rem(x + o, n_inner)}, device_id_type=MESH)

    k_copy = pltpu.make_async_copy(k_hbm, raw.at[0], local_sem.at[1])
    v_copy = pltpu.make_async_copy(v_hbm, raw.at[1], local_sem.at[2])
    l_copy = pltpu.make_async_copy(ld_hbm, ldbuf.at[0, 0, 0:kv], local_sem.at[3])
    q_copy = pltpu.make_async_copy(q_hbm, qbuf, local_sem.at[0])
    g_copy = pltpu.make_async_copy(gain_hbm, gain_ref, local_sem.at[4])
    list_copy = pltpu.make_async_copy(list_hbm, list_ref, local_sem.at[5])
    for copy in (l_copy, k_copy, v_copy, q_copy, list_copy, g_copy):
        copy.start()

    by_head = jnp.where(
        iota((pairs, pairs), 1) == lax.rem(iota((pairs, pairs), 0), tokens) * kv
        + iota((pairs, pairs), 0) // tokens, 1.0, 0.0
    ).astype(BF16)
    l_copy.wait()
    k_copy.wait()
    v_copy.wait()
    apart = dot(by_head, jnp.concatenate([raw[0], raw[1]], axis=1)).astype(BF16)
    for i in range(2):
        for g in range(kv):
            seg[0, i, g] = apart[g * tokens:(g + 1) * tokens, i * width:(i + 1) * width]

    pl.semaphore_wait(barrier, n_inner - 1 + jnp.where(has_next, 1, 0))

    def hop(src, dst, send, recv):
        return pltpu.make_async_remote_copy(
            src_ref=src, dst_ref=dst, send_sem=send, recv_sem=recv,
            device_id={"seq": z + 1}, device_id_type=MESH)

    def across(o, src, dst, send, recv):
        return pltpu.make_async_remote_copy(
            src_ref=src, dst_ref=dst, send_sem=send, recv_sem=recv,
            device_id={"inner": lax.rem(x + o, n_inner)}, device_id_type=MESH)

    def part(ref, i, c):
        per_head = cuts[i] // kv
        if per_head == 0:
            return ref.at[i]
        span = tokens // per_head
        return ref.at[i, c // per_head, pl.ds(c % per_head * span, span)]

    def part_hop(j, i, c):
        return hop(
            part(seg.at[j], i, c), part(seg.at[j + 1], i, c), h_send.at[j],
            (k_recv, v_recv)[i].at[j, c])

    def piece_hop(j):
        return hop(seg.at[j], seg.at[j + 1], h_send.at[j], k_recv.at[j, 0])

    def l_hop(j):
        return hop(
            ldbuf.at[j, 0, 0:kv], ldbuf.at[j + 1, 0, 0:kv], l_send.at[j], l_recv.at[j])

    def part_across(o, j, i, c):
        s = n_inner - o
        recv = c_recv.at[s - 1, j]
        if around and j == last - 1 and i == 0:
            recv = a_recv.at[s - 1]
        return across(
            o, part(seg.at[j], i, c), part(cross.at[s - 1, j], i, c), c_send.at[o - 1, j], recv)

    def half_across(o, j, i, recv):
        s = n_inner - o
        return across(o, seg.at[j, i], cross.at[s - 1, j, i], c_send.at[o - 1, j], recv)

    def keys_around(s):
        return hop(
            cross.at[s - 1, last - 1, 0], cross.at[s - 1, last, 0], a_send.at[s - 1],
            c_recv.at[s - 1, last])

    def send_around():
        for s in others:

            @pl.when(z == last - 1)
            def _():
                half_across(n_inner - s, last - 1, 0, a_recv.at[s - 1]).wait_recv()

            @pl.when((z == last - 1) & first)
            def _():
                keys_around(s).start()

    def piece_across(o, j):
        s = n_inner - o
        return across(o, seg.at[j], cross.at[s - 1, j], c_send.at[o - 1, j], c_recv.at[s - 1, j])

    def l_across(o, j):
        s = n_inner - o
        return across(
            o, ldbuf.at[j, 0, 0:kv], ldbuf.at[j, s, 0:kv], x_send.at[o - 1, j], x_recv.at[s - 1, j])

    def relay_part(j, i, c):
        @pl.when(z >= j)
        def _():
            part_hop(j - 1, i, c).wait_recv()
            if j < last:

                @pl.when(has_next)
                def _():
                    part_hop(j, i, c).start()

            @pl.when(jnp.logical_not(first) if around and j == last and i == 0 else z >= j)
            def _():
                for o in others:
                    part_across(o, j, i, c).start()

    def relay_l(j):
        @pl.when(z >= j)
        def _():
            l_hop(j - 1).wait_recv()
            if j < last:

                @pl.when(has_next)
                def _():
                    l_hop(j).start()

            for o in others:
                l_across(o, j).start()

    @pl.when(has_next)
    def _():
        l_hop(0).start()
        for i in range(2):
            for c in range(cuts[i]):
                part_hop(0, i, c).start()

    for o in others:
        l_across(o, 0).start()

        @pl.when(x + o < n_inner)
        def _():
            piece_across(o, 0).start()

    for s in others:

        @pl.when(x + s < n_inner)
        def _():
            cross[s - 1, 0] = jnp.zeros_like(cross[s - 1, 0])

    for j in range(1, n_seq):

        @pl.when(z < j)
        def _():
            seg[j] = jnp.zeros_like(seg[j])
            for o in others:
                cross[o - 1, j] = jnp.zeros_like(cross[o - 1, j])

    def spread_rows(by_token):
        return jnp.broadcast_to(
            by_token[:, None, :], (tokens, rep, by_token.shape[1])
        ).reshape(rows, by_token.shape[1])

    state[...] = jnp.zeros_like(state)
    after = jnp.where(
        iota((tokens, 2 * tokens), 1) > iota((tokens, 2 * tokens), 0), 1.0, 0.0
    ).astype(BF16)

    def decays():
        ld = ldbuf[0, 0]
        seen = iota((tokens, tokens), 0) >= iota((tokens, tokens), 1)
        upto = jnp.where(iota((tokens, tokens), 0) <= iota((tokens, tokens), 1), 1.0, 0.0)
        cum_lane = dot(ld, upto, precision=HIGH)
        ld_rows = jnp.concatenate(
            [jnp.broadcast_to(ld[g:g + 1, :], (width, tokens)) for g in range(kv)], axis=0)
        cum_all = dot(jnp.where(seen, 1.0, 0.0), ld_rows, ((1,), (1,)), HIGH)
        for g in range(kv):
            cum = cum_all[:, g * width:(g + 1) * width]
            emat[g] = spread_rows(jnp.exp(cum))
            wmat[g] = jnp.where(
                seen, jnp.exp(jnp.minimum(cum - cum_lane[g:g + 1, :], 0.0)), 0.0)

    def place(s):
        return lax.rem(x + s, n_inner)

    def later_than(j, s):
        total = jnp.zeros((LD_ROWS, tokens), F32)
        for r in range(n_inner):
            if j == 0 and r > 0:
                total = total + jnp.where(
                    (place(r) > place(s)) & (place(r) < x), ldbuf[0, r], 0.0)
            elif j > 0:
                if r != s:
                    total = total + jnp.where(place(r) > place(s), ldbuf[j, r], 0.0)
                if r > 0:
                    total = total + jnp.where(place(r) < x, ldbuf[0, r], 0.0)
                for i in range(1, j):
                    total = total + ldbuf[i, r]
        return total

    def weigh_pieces(pieces):
        both = jnp.concatenate([
            jnp.concatenate([ldbuf[j, s], later_than(j, s)], axis=1) for j, s in pieces], axis=0)
        tail = dot(
            jnp.concatenate([after] * 3, axis=1), jnp.concatenate(thirds(both), axis=1),
            ((1,), (1,)))
        weight = jnp.exp(tail)
        for n, (j, s) in enumerate(pieces):
            for g in range(kv):
                col = weight[:, n * LD_ROWS + g:n * LD_ROWS + g + 1]
                if j == 0:
                    col = jnp.where(place(s) < x, col, 0.0)
                cols[j % 3, s, g] = jnp.broadcast_to(col, (tokens, width))

    def absorb(pieces):
        for g in range(kv):
            left, right = [], []
            for j, s in pieces:
                piece = seg.at[j] if s == 0 else cross.at[s - 1, j]
                k_g = piece[0, g]
                hi, lo = halves(piece[1, g].astype(F32) * cols[j % 3, s, g])
                left += [k_g, k_g]
                right += [hi, lo]
            state[g] += dot(
                jnp.concatenate(left, axis=0), jnp.concatenate(right, axis=0), ((0,), (0,)))

    def row_of(j):
        return [(j, s) for s in range(1 if j == 0 else 0, n_inner)]

    def arrive_l(j):
        for s in others:

            @pl.when(z >= j)
            def _():
                l_across(n_inner - s, j).wait_recv()

    def arrive(j):
        for s in others:
            @pl.when((x + s >= n_inner) if j == 0 else (z >= j))
            def _():
                if around and j == last - 1:
                    half_across(n_inner - s, j, 1, c_recv.at[s - 1, j]).wait_recv()

                    @pl.when(z == last)
                    def _():
                        half_across(n_inner - s, j, 0, a_recv.at[s - 1]).wait_recv()

                else:
                    piece_across(n_inner - s, j).wait_recv()


    def visibility():
        list_copy.wait()
        lane = iota((1, keys_all), 1)
        key_block = (
            ((z - lane // tokens) * n_inner + x) * per_piece + lax.rem(lane, tokens) // BLK
        )
        listed = list_ref[...]
        for b in range(per_piece):
            member = key_block == listed[b:b + 1, 0:1]
            for i in range(1, listed.shape[1]):
                member = jnp.logical_or(member, key_block == listed[b:b + 1, i:i + 1])
            vis[b:b + 1, :] = jnp.where(member, 0.0, NEVER)

    def take_queries():
        q_copy.wait()
        qf = qbuf[...].astype(F32)
        for g in range(kv):
            qs[g] = qf[:, g * rep:(g + 1) * rep, :].reshape(rows, width).astype(BF16)

    half = BLK * rep
    scale = width ** (-0.5) * LOG2E

    def shown(s, j):
        cut = slice(j * tokens, (j + 1) * tokens)
        return jnp.concatenate(
            [s[b * half:(b + 1) * half] * scale + vis[b:b + 1, cut] for b in range(per_piece)],
            axis=0)

    def own_piece(g):
        plain = dot(qs[g], seg[0, 0, g], ((1,), (1,)))
        past = iota((rows, tokens), 0) // rep >= iota((rows, tokens), 1)
        score[g, :, 0:tokens] = jnp.where(past, shown(plain, 0), NEVER)
        hi, lo = halves(plain * spread_rows(wmat[g]))
        v_g = seg[0, 1, g]
        lin[g] = dot(
            jnp.concatenate([hi, lo], axis=1), jnp.concatenate([v_g, v_g], axis=0))

    def score_piece(j, those):
        for g in those:
            s = dot(qs[g], seg[j, 0, g], ((1,), (1,)))
            score[g, :, j * tokens:(j + 1) * tokens] = shown(s, j)

    def weigh(g, at):
        s = score[g, at, :]
        top = jnp.max(s, axis=1, keepdims=True)
        expo = jnp.exp2(s - top)
        denom = jnp.sum(expo, axis=1, keepdims=True)
        prob[g, at, :] = expo.astype(BF16)
        inv[g, at, :] = jnp.broadcast_to(1.0 / denom, (s.shape[0], width))

    def sparse(g):
        v_g = jnp.concatenate([seg[j, 1, g] for j in range(n_seq)], axis=0)
        sp[g] = dot(prob[g], v_g) * inv[g]

    decays()
    take_queries()
    visibility()

    for g in range(kv):
        own_piece(g)

    weighing = [
        functools.partial(weigh, g, slice(b * half, (b + 1) * half))
        for g in range(kv) for b in range(per_piece)
    ]
    for j in range(1, n_seq):
        if j == 1 or j < last:
            relay_l(j)
        early = 0
        for c in range(cuts[0]):
            relay_part(j, 0, c)
            if j == last > 1 and cuts[0] == kv:
                if c == kv - 1:
                    early = 1
                    relay_part(j, 1, 0)
                score_piece(j, [c])
        arrive_l(j - 1)
        if early == 0:
            score_piece(j, range(kv))
        if j < last:
            weigh_pieces(row_of(j - 1))
        for c in range(cuts[1]):
            if c >= early:
                relay_part(j, 1, c)
        if j == last - 1:
            relay_l(last)
        if j == last:
            if around:
                send_around()
            weigh_pieces(row_of(j - 1))
            for item in weighing:
                item()
        if 1 < j < last:
            arrive(j - 2)
            absorb(row_of(j - 2))
    if n_seq == 1:
        for item in weighing:
            item()
    if last > 1:
        arrive(last - 2)
    for g in range(kv):
        sparse(g)
    if last > 1:
        absorb(row_of(last - 2) + [(last - 1, 0)])
    arrive_l(last)
    weigh_pieces(row_of(last))
    g_copy.wait()
    gains = gain_ref[...] * width ** 0.5

    for j in range(last):

        @pl.when((z >= j) & has_next)
        def _():
            piece_hop(j).wait_send()
            l_hop(j).wait_send()

    if around:

        @pl.when((z == last - 1) & first)
        def _():
            for s in others:
                keys_around(s).wait_send()

    for o in others:
        for j in range(last):

            @pl.when(z >= j)
            def _():
                l_across(o, j).wait_send()

            @pl.when((x + o < n_inner) if j == 0 else (z >= j))
            def _():
                piece_across(o, j).wait_send()

    if last > 0:
        arrive(last - 1)
        absorb([(last - 1, s) for s in others if last > 0] + [(last, 0)])

    arrive(last)
    absorb([(last, s) for s in others])
    done = []
    for g in range(kv):
        hi, lo = halves(state[g])
        q_g = qs[g]
        inter = dot(
            jnp.concatenate([q_g, q_g], axis=1), jnp.concatenate([hi, lo], axis=0))
        linear = lin[g] + inter * emat[g]
        norm = lax.rsqrt(jnp.sum(linear * linear, axis=1, keepdims=True) + width * 1e-6)
        scaled = (linear * norm).reshape(tokens, rep, width) * gains[g * rep:(g + 1) * rep, :][None]
        done.append(scaled + sp[g].reshape(tokens, rep, width))
    out_ref[...] = jnp.concatenate(done, axis=1).astype(out_ref.dtype)

    for o in others:

        @pl.when(z >= last)
        def _():
            l_across(o, last).wait_send()
            if around:

                @pl.when(first)
                def _():
                    half_across(o, last, 1, c_recv.at[n_inner - o - 1, last]).wait_send()

                @pl.when(jnp.logical_not(first))
                def _():
                    piece_across(o, last).wait_send()

            else:
                piece_across(o, last).wait_send()


def shards(n_seq, n_inner, queries, keys, values, log_decay, gain, block_list):
    tokens, heads, width = queries.shape
    kv = keys.shape[1]
    rows = tokens * (heads // kv)
    pairs = tokens * kv
    keys_all = n_seq * tokens
    cuts = (kv, 2 * kv) if n_seq * n_inner <= 16 else (1, 1)
    side, hops = max(n_inner - 1, 1), max(n_seq - 1, 1)
    anywhere = pl.BlockSpec(memory_space=pl.ANY)
    dma = pltpu.SemaphoreType.DMA
    return pl.pallas_call(
        functools.partial(kernel, n_seq, n_inner, kv, cuts),
        out_shape=pltpu.VMEM(queries.shape, queries.dtype),
        in_specs=[anywhere] * 6,
        out_specs=pl.BlockSpec(memory_space=pltpu.VMEM),
        scratch_shapes=[
            pltpu.VMEM(gain.shape, F32),
            pltpu.VMEM(block_list.shape, jnp.int32),
            pltpu.VMEM(queries.shape, BF16),
            pltpu.VMEM((2, pairs, width), BF16),
            pltpu.VMEM((n_seq, 2, kv, tokens, width), BF16),
            pltpu.VMEM((side, n_seq, 2, kv, tokens, width), BF16),
            pltpu.VMEM((n_seq, n_inner, LD_ROWS, tokens), F32),
            pltpu.VMEM((kv, rows, width), BF16),
            pltpu.VMEM((block_list.shape[0], keys_all), F32),
            pltpu.VMEM((kv, tokens, tokens), F32),
            pltpu.VMEM((kv, rows, width), F32),
            pltpu.VMEM((3, n_inner, kv, tokens, width), F32),
            pltpu.VMEM((kv, rows, keys_all), F32),
            pltpu.VMEM((kv, rows, keys_all), BF16),
            pltpu.VMEM((kv, rows, width), F32),
            pltpu.VMEM((kv, rows, width), F32),
            pltpu.VMEM((kv, rows, width), F32),
            pltpu.VMEM((kv, width, width), F32),
            dma((6,)),
            dma((hops, cuts[0])), dma((hops, cuts[1])), dma((hops,)),
            dma((hops,)), dma((hops,)), dma((side, n_seq)), dma((side, n_seq)),
            dma((side, n_seq)), dma((side, n_seq)), dma((side,)), dma((side,)),
        ],
        compiler_params=pltpu.CompilerParams(collective_id=0, has_side_effects=True),
        name="prefill",
    )(
        queries, keys.reshape(pairs, width), values.reshape(pairs, width),
        log_decay.T, gain, block_list,
    )


def solution(mesh):
    return jax.shard_map(
        functools.partial(shards, mesh.shape["seq"], mesh.shape["inner"]),
        mesh=mesh,
        in_specs=(
            P(("groups", "seq", "inner"), "head", None),
            P(("groups", "seq", "inner"), "head", None),
            P(("groups", "seq", "inner"), "head", None),
            P(("groups", "seq", "inner"), "head"),
            P("head", None),
            P(("groups", "seq", "inner"), None),
        ),
        out_specs=P(("groups", "seq", "inner"), "head", None),
        check_vma=False,
    )
```

```python
import functools

import jax
import jax.numpy as jnp
from jax import lax
from jax.experimental import pallas as pl
from jax.experimental.pallas import tpu as pltpu
from jax.sharding import PartitionSpec as P

BLK = 64
HIGH = lax.Precision.HIGHEST
MESH = pl.DeviceIdType.MESH
LD_ROWS = 8
F32 = jnp.float32
BF16 = jnp.bfloat16
LOG2E = 1.4426950408889634
NEVER = -1e30


def iota(shape, dim):
    return lax.broadcasted_iota(jnp.int32, shape, dim)


def dot(a, b, dims=((1,), (0,)), precision=None):
    return lax.dot_general(
        a, b, (dims, ((), ())), precision=precision, preferred_element_type=F32
    )


def halves(x):
    hi = x.astype(BF16)
    return hi, (x - hi.astype(F32)).astype(BF16)


def thirds(x):
    hi = x.astype(BF16)
    rest = x - hi.astype(F32)
    mid = rest.astype(BF16)
    return hi, mid, (rest - mid.astype(F32)).astype(BF16)


def kernel(
    n_seq, n_inner, kv, cuts,
    q_hbm, k_hbm, v_hbm, ld_hbm, gain_hbm, list_hbm,
    out_ref,
    gain_ref, list_ref, qbuf, raw, seg, cross, ldbuf, qs, vis, wmat, emat, cols,
    score, prob, inv, lin, sp, state,
    local_sem, k_recv, v_recv, h_send, l_send, l_recv, x_send, x_recv, c_send, c_recv, a_send,
):
    z = lax.axis_index("seq")
    x = lax.axis_index("inner")
    tokens, heads, width = qbuf.shape
    rep = heads // kv
    rows = tokens * rep
    pairs = tokens * kv
    per_piece = tokens // BLK
    keys_all = n_seq * tokens
    has_next, has_last = z < n_seq - 1, z > 0
    others = range(1, n_inner)
    last = n_seq - 1
    around = last > 2
    first = lax.axis_index("head") == 0
    turns = (z == last - 1) & first if around else z < 0
    skips = (z == last) & first if around else z < 0

    barrier = pltpu.get_barrier_semaphore()

    ldbuf[...] = jnp.zeros_like(ldbuf)

    @pl.when(has_last)
    def _():
        pl.semaphore_signal(barrier, inc=1, device_id={"seq": z - 1}, device_id_type=MESH)

    for o in others:
        pl.semaphore_signal(
            barrier, inc=1, device_id={"inner": lax.rem(x + o, n_inner)}, device_id_type=MESH)

    k_copy = pltpu.make_async_copy(k_hbm, raw.at[0], local_sem.at[1])
    v_copy = pltpu.make_async_copy(v_hbm, raw.at[1], local_sem.at[2])
    l_copy = pltpu.make_async_copy(ld_hbm, ldbuf.at[0, 0, 0:kv], local_sem.at[3])
    q_copy = pltpu.make_async_copy(q_hbm, qbuf, local_sem.at[0])
    g_copy = pltpu.make_async_copy(gain_hbm, gain_ref, local_sem.at[4])
    list_copy = pltpu.make_async_copy(list_hbm, list_ref, local_sem.at[5])
    for copy in (l_copy, k_copy, v_copy, q_copy, list_copy, g_copy):
        copy.start()

    by_head = jnp.where(
        iota((pairs, pairs), 1) == lax.rem(iota((pairs, pairs), 0), tokens) * kv
        + iota((pairs, pairs), 0) // tokens, 1.0, 0.0
    ).astype(BF16)
    l_copy.wait()
    k_copy.wait()
    v_copy.wait()
    apart = dot(by_head, jnp.concatenate([raw[0], raw[1]], axis=1)).astype(BF16)
    for i in range(2):
        for g in range(kv):
            seg[0, i, g] = apart[g * tokens:(g + 1) * tokens, i * width:(i + 1) * width]

    pl.semaphore_wait(barrier, n_inner - 1 + jnp.where(has_next, 1, 0))

    def hop(src, dst, send, recv):
        return pltpu.make_async_remote_copy(
            src_ref=src, dst_ref=dst, send_sem=send, recv_sem=recv,
            device_id={"seq": z + 1}, device_id_type=MESH)

    def across(o, src, dst, send, recv):
        return pltpu.make_async_remote_copy(
            src_ref=src, dst_ref=dst, send_sem=send, recv_sem=recv,
            device_id={"inner": lax.rem(x + o, n_inner)}, device_id_type=MESH)

    def part(ref, i, c):
        per_head = cuts[i] // kv
        if per_head == 0:
            return ref.at[i]
        span = tokens // per_head
        return ref.at[i, c // per_head, pl.ds(c % per_head * span, span)]

    def part_hop(j, i, c):
        return hop(
            part(seg.at[j], i, c), part(seg.at[j + 1], i, c), h_send.at[j],
            (k_recv, v_recv)[i].at[j, c])

    def piece_hop(j):
        return hop(seg.at[j], seg.at[j + 1], h_send.at[j], k_recv.at[j, 0])

    def l_hop(j):
        return hop(
            ldbuf.at[j, 0, 0:kv], ldbuf.at[j + 1, 0, 0:kv], l_send.at[j], l_recv.at[j])

    def part_across(o, j, i, c):
        s = n_inner - o
        return across(
            o, part(seg.at[j], i, c), part(cross.at[s - 1, j], i, c), c_send.at[o - 1, j],
            c_recv.at[s - 1, j])

    def piece_across(o, j):
        s = n_inner - o
        return across(o, seg.at[j], cross.at[s - 1, j], c_send.at[o - 1, j], c_recv.at[s - 1, j])

    def l_across(o, j):
        s = n_inner - o
        return across(
            o, ldbuf.at[j, 0, 0:kv], ldbuf.at[j, s, 0:kv], x_send.at[o - 1, j], x_recv.at[s - 1, j])

    def relay_part(j, i, c):
        @pl.when(z >= j)
        def _():
            part_hop(j - 1, i, c).wait_recv()
            if j < last:

                @pl.when(has_next)
                def _():
                    part_hop(j, i, c).start()

            @pl.when(jnp.logical_not(skips) if j == 1 else z >= j)
            def _():
                for o in others:
                    part_across(o, j, i, c).start()

    def piece_around(s):
        return hop(cross.at[s - 1, 0], cross.at[s - 1, 1], a_send.at[s - 1], c_recv.at[s - 1, 1])

    def relay_l(j):
        @pl.when(z >= j)
        def _():
            l_hop(j - 1).wait_recv()
            if j < last:

                @pl.when(has_next)
                def _():
                    l_hop(j).start()

            for o in others:
                l_across(o, j).start()

    @pl.when(has_next)
    def _():
        l_hop(0).start()
        for i in range(2):
            for c in range(cuts[i]):
                part_hop(0, i, c).start()

    for o in others:
        l_across(o, 0).start()

        @pl.when((x + o < n_inner) | turns)
        def _():
            piece_across(o, 0).start()

    for s in others:

        @pl.when((x + s < n_inner) & jnp.logical_not(turns))
        def _():
            cross[s - 1, 0] = jnp.zeros_like(cross[s - 1, 0])

    for j in range(1, n_seq):

        @pl.when(z < j)
        def _():
            seg[j] = jnp.zeros_like(seg[j])
            for o in others:
                cross[o - 1, j] = jnp.zeros_like(cross[o - 1, j])

    def spread_rows(by_token):
        return jnp.broadcast_to(
            by_token[:, None, :], (tokens, rep, by_token.shape[1])
        ).reshape(rows, by_token.shape[1])

    state[...] = jnp.zeros_like(state)
    after = jnp.where(
        iota((tokens, 2 * tokens), 1) > iota((tokens, 2 * tokens), 0), 1.0, 0.0
    ).astype(BF16)

    def decays():
        ld = ldbuf[0, 0]
        seen = iota((tokens, tokens), 0) >= iota((tokens, tokens), 1)
        upto = jnp.where(iota((tokens, tokens), 0) <= iota((tokens, tokens), 1), 1.0, 0.0)
        cum_lane = dot(ld, upto, precision=HIGH)
        ld_rows = jnp.concatenate(
            [jnp.broadcast_to(ld[g:g + 1, :], (width, tokens)) for g in range(kv)], axis=0)
        cum_all = dot(jnp.where(seen, 1.0, 0.0), ld_rows, ((1,), (1,)), HIGH)
        for g in range(kv):
            cum = cum_all[:, g * width:(g + 1) * width]
            emat[g] = spread_rows(jnp.exp(cum))
            wmat[g] = jnp.where(
                seen, jnp.exp(jnp.minimum(cum - cum_lane[g:g + 1, :], 0.0)), 0.0)

    def place(s):
        return lax.rem(x + s, n_inner)

    def later_than(j, s):
        total = jnp.zeros((LD_ROWS, tokens), F32)
        for r in range(n_inner):
            if j == 0 and r > 0:
                total = total + jnp.where(
                    (place(r) > place(s)) & (place(r) < x), ldbuf[0, r], 0.0)
            elif j > 0:
                if r != s:
                    total = total + jnp.where(place(r) > place(s), ldbuf[j, r], 0.0)
                if r > 0:
                    total = total + jnp.where(place(r) < x, ldbuf[0, r], 0.0)
                for i in range(1, j):
                    total = total + ldbuf[i, r]
        return total

    def weigh_pieces(pieces):
        both = jnp.concatenate([
            jnp.concatenate([ldbuf[j, s], later_than(j, s)], axis=1) for j, s in pieces], axis=0)
        tail = dot(
            jnp.concatenate([after] * 3, axis=1), jnp.concatenate(thirds(both), axis=1),
            ((1,), (1,)))
        weight = jnp.exp(tail)
        for n, (j, s) in enumerate(pieces):
            for g in range(kv):
                col = weight[:, n * LD_ROWS + g:n * LD_ROWS + g + 1]
                if j == 0:
                    col = jnp.where(place(s) < x, col, 0.0)
                cols[j % 3, s, g] = jnp.broadcast_to(col, (tokens, width))

    def absorb(pieces):
        for g in range(kv):
            left, right = [], []
            for j, s in pieces:
                piece = seg.at[j] if s == 0 else cross.at[s - 1, j]
                k_g = piece[0, g]
                hi, lo = halves(piece[1, g].astype(F32) * cols[j % 3, s, g])
                left += [k_g, k_g]
                right += [hi, lo]
            state[g] += dot(
                jnp.concatenate(left, axis=0), jnp.concatenate(right, axis=0), ((0,), (0,)))

    def row_of(j):
        return [(j, s) for s in range(1 if j == 0 else 0, n_inner)]

    def arrive_l(j):
        for s in others:

            @pl.when(z >= j)
            def _():
                l_across(n_inner - s, j).wait_recv()

    def arrive(j):
        for s in others:
            @pl.when((x + s >= n_inner) | turns if j == 0 else z >= j)
            def _():
                piece_across(n_inner - s, j).wait_recv()


    def visibility():
        list_copy.wait()
        lane = iota((1, keys_all), 1)
        key_block = (
            ((z - lane // tokens) * n_inner + x) * per_piece + lax.rem(lane, tokens) // BLK
        )
        listed = list_ref[...]
        for b in range(per_piece):
            member = key_block == listed[b:b + 1, 0:1]
            for i in range(1, listed.shape[1]):
                member = jnp.logical_or(member, key_block == listed[b:b + 1, i:i + 1])
            vis[b:b + 1, :] = jnp.where(member, 0.0, NEVER)

    def take_queries():
        q_copy.wait()
        qf = qbuf[...].astype(F32)
        for g in range(kv):
            qs[g] = qf[:, g * rep:(g + 1) * rep, :].reshape(rows, width).astype(BF16)

    half = BLK * rep
    scale = width ** (-0.5) * LOG2E

    def shown(s, j):
        cut = slice(j * tokens, (j + 1) * tokens)
        return jnp.concatenate(
            [s[b * half:(b + 1) * half] * scale + vis[b:b + 1, cut] for b in range(per_piece)],
            axis=0)

    def own_piece(g):
        plain = dot(qs[g], seg[0, 0, g], ((1,), (1,)))
        past = iota((rows, tokens), 0) // rep >= iota((rows, tokens), 1)
        score[g, :, 0:tokens] = jnp.where(past, shown(plain, 0), NEVER)
        hi, lo = halves(plain * spread_rows(wmat[g]))
        v_g = seg[0, 1, g]
        lin[g] = dot(
            jnp.concatenate([hi, lo], axis=1), jnp.concatenate([v_g, v_g], axis=0))

    def score_piece(j, those):
        for g in those:
            s = dot(qs[g], seg[j, 0, g], ((1,), (1,)))
            score[g, :, j * tokens:(j + 1) * tokens] = shown(s, j)

    def weigh(g, at):
        s = score[g, at, :]
        top = jnp.max(s, axis=1, keepdims=True)
        expo = jnp.exp2(s - top)
        denom = jnp.sum(expo, axis=1, keepdims=True)
        prob[g, at, :] = expo.astype(BF16)
        inv[g, at, :] = jnp.broadcast_to(1.0 / denom, (s.shape[0], width))

    def sparse(g):
        v_g = jnp.concatenate([seg[j, 1, g] for j in range(n_seq)], axis=0)
        sp[g] = dot(prob[g], v_g) * inv[g]

    decays()
    take_queries()
    visibility()

    for g in range(kv):
        own_piece(g)

    weighing = [
        functools.partial(weigh, g, slice(b * half, (b + 1) * half))
        for g in range(kv) for b in range(per_piece)
    ]
    for j in range(1, n_seq):
        if j == 1 or j < last:
            relay_l(j)
        early = 0
        for c in range(cuts[0]):
            relay_part(j, 0, c)
            if j == last > 1 and cuts[0] == kv:
                if c == kv - 1:
                    early = 1
                    relay_part(j, 1, 0)
                score_piece(j, [c])
        arrive_l(j - 1)
        if early == 0:
            score_piece(j, range(kv))
        if j < last:
            weigh_pieces(row_of(j - 1))
        for c in range(cuts[1]):
            if c >= early:
                relay_part(j, 1, c)
        if j == last - 1:
            relay_l(last)
        if j == last:
            weigh_pieces(row_of(j - 1))
            for item in weighing:
                item()
        if 1 < j < last:
            arrive(j - 2)
            if around and j == last - 1:

                @pl.when(turns)
                def _():
                    for s in others:
                        piece_around(s).start()

            absorb(row_of(j - 2))
    if n_seq == 1:
        for item in weighing:
            item()
    for g in range(kv):
        sparse(g)
    if last > 1:
        absorb([(j, 0) for j in range(max(last - 2, 1), last)])
    arrive_l(last)
    weigh_pieces(row_of(last))
    g_copy.wait()
    gains = gain_ref[...] * width ** 0.5

    for j in range(last):

        @pl.when((z >= j) & has_next)
        def _():
            piece_hop(j).wait_send()
            l_hop(j).wait_send()

    if around:

        @pl.when(turns)
        def _():
            for s in others:
                piece_around(s).wait_send()

    for o in others:
        for j in range(last):

            @pl.when(z >= j)
            def _():
                l_across(o, j).wait_send()

            @pl.when(
                (x + o < n_inner) | turns if j == 0
                else (z >= j) & jnp.logical_not(skips) if j == 1 else z >= j)
            def _():
                piece_across(o, j).wait_send()

    if last > 0:
        two = range(max(last - 2, 0), last)
        for j in two:
            arrive(j)
        absorb([(j, s) for j in two for s in others] + [(last, 0)])

    arrive(last)
    absorb([(last, s) for s in others])
    done = []
    for g in range(kv):
        hi, lo = halves(state[g])
        q_g = qs[g]
        inter = dot(
            jnp.concatenate([q_g, q_g], axis=1), jnp.concatenate([hi, lo], axis=0))
        linear = lin[g] + inter * emat[g]
        norm = lax.rsqrt(jnp.sum(linear * linear, axis=1, keepdims=True) + width * 1e-6)
        scaled = (linear * norm).reshape(tokens, rep, width) * gains[g * rep:(g + 1) * rep, :][None]
        done.append(scaled + sp[g].reshape(tokens, rep, width))
    out_ref[...] = jnp.concatenate(done, axis=1).astype(out_ref.dtype)

    for o in others:

        @pl.when(z >= last)
        def _():
            l_across(o, last).wait_send()
            piece_across(o, last).wait_send()


def shards(n_seq, n_inner, queries, keys, values, log_decay, gain, block_list):
    tokens, heads, width = queries.shape
    kv = keys.shape[1]
    rows = tokens * (heads // kv)
    pairs = tokens * kv
    keys_all = n_seq * tokens
    cuts = (kv, kv) if n_seq * n_inner <= 16 else (1, 1)
    side, hops = max(n_inner - 1, 1), max(n_seq - 1, 1)
    anywhere = pl.BlockSpec(memory_space=pl.ANY)
    dma = pltpu.SemaphoreType.DMA
    return pl.pallas_call(
        functools.partial(kernel, n_seq, n_inner, kv, cuts),
        out_shape=pltpu.VMEM(queries.shape, queries.dtype),
        in_specs=[anywhere] * 6,
        out_specs=pl.BlockSpec(memory_space=pltpu.VMEM),
        scratch_shapes=[
            pltpu.VMEM(gain.shape, F32),
            pltpu.VMEM(block_list.shape, jnp.int32),
            pltpu.VMEM(queries.shape, BF16),
            pltpu.VMEM((2, pairs, width), BF16),
            pltpu.VMEM((n_seq, 2, kv, tokens, width), BF16),
            pltpu.VMEM((side, n_seq, 2, kv, tokens, width), BF16),
            pltpu.VMEM((n_seq, n_inner, LD_ROWS, tokens), F32),
            pltpu.VMEM((kv, rows, width), BF16),
            pltpu.VMEM((block_list.shape[0], keys_all), F32),
            pltpu.VMEM((kv, tokens, tokens), F32),
            pltpu.VMEM((kv, rows, width), F32),
            pltpu.VMEM((3, n_inner, kv, tokens, width), F32),
            pltpu.VMEM((kv, rows, keys_all), F32),
            pltpu.VMEM((kv, rows, keys_all), BF16),
            pltpu.VMEM((kv, rows, width), F32),
            pltpu.VMEM((kv, rows, width), F32),
            pltpu.VMEM((kv, rows, width), F32),
            pltpu.VMEM((kv, width, width), F32),
            dma((6,)),
            dma((hops, cuts[0])), dma((hops, cuts[1])), dma((hops,)),
            dma((hops,)), dma((hops,)), dma((side, n_seq)), dma((side, n_seq)),
            dma((side, n_seq)), dma((side, n_seq)), dma((side,)),
        ],
        compiler_params=pltpu.CompilerParams(collective_id=0, has_side_effects=True),
        name="prefill",
    )(
        queries, keys.reshape(pairs, width), values.reshape(pairs, width),
        log_decay.T, gain, block_list,
    )


def solution(mesh):
    return jax.shard_map(
        functools.partial(shards, mesh.shape["seq"], mesh.shape["inner"]),
        mesh=mesh,
        in_specs=(
            P(("groups", "seq", "inner"), "head", None),
            P(("groups", "seq", "inner"), "head", None),
            P(("groups", "seq", "inner"), "head", None),
            P(("groups", "seq", "inner"), "head"),
            P("head", None),
            P(("groups", "seq", "inner"), None),
        ),
        out_specs=P(("groups", "seq", "inner"), "head", None),
        check_vma=False,
    )
```
